128 devices in a mesh: head: 4 (over z), page: 32 (over y, x, core).
Axes of the slice: x: 4, y: 4, z: 4, core: 2. Of those that a mesh axis runs over, the one named last changes fastest.
Arguments:
- hidden: bfloat16 [4096, 4096], P('page', 'head'), may hold values from -6 to 6
- group_qkv: bfloat16 [4096, 6144], P('page', 'head'), may hold values from -2400 to 2400
- mlp_branch: bfloat16 [4096, 4096], P('page', 'head'), may hold values from -6 to 6
- key_cache: bfloat16 [416, 128, 2048], P('page', None, 'head'), may hold values from -6 to 6
- paged_value_cache: bfloat16 [416, 128, 2048], P('page', None, 'head'), may hold values from -6 to 6
- cache_lengths: int32 [8], replicated, may hold values from 2 to 4096, as said below
- page_table: int32 [8, 36], replicated, may hold values from 0 to 415, as said below
- dense_weight: bfloat16 [2048, 4096], P('head'), may hold values from -0.125 to 0.125
- dense_bias: float32 [4096], replicated, may hold values from -3 to 3
- norm_gain: float32 [4096], replicated, may hold values from 0.1 to 1.9
- norm_bias: float32 [4096], replicated, may hold values from -3 to 3
- qkv_weight: bfloat16 [4096, 6144], P(None, 'head'), may hold values from -0.09375 to 0.09375
- qkv_bias: float32 [6144], P('head'), may hold values from -3 to 3
Outputs:
- new_hidden: bfloat16 [4096, 4096], P('page', 'head')
- next_qkv: bfloat16 [4096, 6144], P('page', 'head')
- key_out: bfloat16 [416, 128, 2048], P('page', None, 'head')
- value_out: bfloat16 [416, 128, 2048], P('page', None, 'head')
The draws below stay inside these ranges and needn't reach their ends.
Inputs may be any that keep to these rules, and one draw needn't show every extreme that they name: `cache_lengths`: one request has exactly 4096 cached positions and another exactly 2. `page_table`: all entries are distinct slots; slot s lies on index s // 13 of page.
All inputs are finite; a program needn't handle non-finite values.
Results may differ from the reference program's by a relative error of at most 0.0075.
Values may be sent and summed in bfloat16 or wider, within the bound.
No kernel may reach another device: no remote copies, remote signals or barrier semaphores. Data moves between devices by JAX's collectives and lax.ppermute only.
A program may use at most 192 MiB of HBM per device.

```python
import math
import jax
import jax.numpy as jnp
from jax import lax

D = 4096
HALF_HEADS = 16
HEAD_SIZE = 128
ROT = 32
PAGE_TOKENS = 128
GROUP = 512
MAXLEN = 4096
TOKENS = 4096
REQS = 8
MAXP = 36
TOTAL_SLOTS = 416


def table_of(key):
    permuted_slots = jax.random.permutation(jax.random.fold_in(key, 11), TOTAL_SLOTS)
    return permuted_slots[:REQS * MAXP].reshape(REQS, MAXP).astype(jnp.int32)


def keys_of(key):
    gaussian_sample = jax.random.truncated_normal(jax.random.fold_in(key, 14), -6.0, 6.0, (TOTAL_SLOTS, PAGE_TOKENS, HALF_HEADS * HEAD_SIZE), jnp.float32)
    return gaussian_sample


def draw_page_table(key, part):
    return table_of(key)


def draw_cache_lengths(key, part):
    base_lengths = jax.random.randint(jax.random.fold_in(key, 12), (REQS,), 2, MAXLEN + 1)
    shuffled = jax.random.permutation(jax.random.fold_in(key, 13), REQS)
    return base_lengths.at[shuffled[0]].set(MAXLEN).at[shuffled[1]].set(2).astype(jnp.int32)


def draw_key_cache(key, part):
    return keys_of(key).astype(jnp.bfloat16)


def draw_group_qkv(key, part):
    gaussian_sample = jax.random.truncated_normal(jax.random.fold_in(key, 15), -6.0, 6.0, (REQS, GROUP, HALF_HEADS, 3, HEAD_SIZE), jnp.float32)
    return gaussian_sample.reshape(TOKENS, HALF_HEADS * 3 * HEAD_SIZE).astype(jnp.bfloat16)


def steps_of(stream_key, extent, shards, least, largest):
    def one(dim, shards_of):
        steps = jax.random.uniform(jax.random.fold_in(jax.random.fold_in(stream_key, 6), dim), (shards_of,), jnp.float32, least / len(shards), largest / len(shards))
        return jnp.repeat(jnp.exp(steps), extent[dim] // shards_of).reshape((-1,) + (1,) * (len(extent) - dim - 1))

    factor_of = one(*shards[0])
    for cut in shards[1:]:
        factor_of = factor_of * one(*cut)
    return factor_of


def normal_values(rng, extent, spread, limit, cuts=(), held_as=jnp.bfloat16):
    gain = steps_of(rng, extent, cuts, -0.22, 0.18) if cuts else 1.0
    values = jax.random.normal(rng, extent, jnp.float32) * spread * gain
    return jnp.minimum(jnp.maximum(values, -limit), limit).astype(held_as)


def setup_inputs(seed: int = 0) -> dict:
    splits = jax.random.split(jax.random.key(seed), 14)
    return {
        "hidden": normal_values(splits[0], (TOKENS, D), 1.0, 6.0, ((0, 32), (1, 4))),
        "group_qkv": draw_group_qkv(jax.random.fold_in(splits[13], 71), 0),
        "mlp_branch": normal_values(splits[2], (TOKENS, D), 1.0, 6.0, ((0, 32), (1, 4))),
        "key_cache": draw_key_cache(jax.random.fold_in(splits[13], 71), 0),
        "paged_value_cache": normal_values(splits[4], (TOTAL_SLOTS, PAGE_TOKENS, HALF_HEADS * HEAD_SIZE), 1.0, 6.0, ((0, 32), (2, 4))),
        "cache_lengths": draw_cache_lengths(jax.random.fold_in(splits[13], 71), 0),
        "page_table": draw_page_table(jax.random.fold_in(splits[13], 71), 0),
        "dense_weight": normal_values(splits[7], (HALF_HEADS * HEAD_SIZE, D), (HALF_HEADS * HEAD_SIZE) ** -0.5, 0.125, ((0, 4),)),
        "dense_bias": normal_values(splits[8], (D,), 0.5, 3.0, (), jnp.float32),
        "norm_gain": jnp.clip(1.0 + 0.18 * jax.random.normal(splits[9], (D,), jnp.float32), 0.1, 1.9),
        "norm_bias": normal_values(splits[10], (D,), 0.5, 3.0, (), jnp.float32),
        "qkv_weight": normal_values(splits[11], (D, HALF_HEADS * 3 * HEAD_SIZE), D ** -0.5, 0.09375, ((1, 4),)),
        "qkv_bias": normal_values(splits[12], (HALF_HEADS * 3 * HEAD_SIZE,), 0.5, 3.0, ((0, 4),), jnp.float32),
    }


def rotate_rows(inputs, positions):
    half_rot = ROT // 2
    inverse = 1.0 / 10000.0 ** (jnp.arange(0, ROT, 2, dtype=jnp.float32) / ROT)
    angles = positions.astype(jnp.float32)[:, None] * inverse[None, :]
    cosine = jnp.cos(angles)[:, None, :]
    sine_part = jnp.sin(angles)[:, None, :]
    first_half = inputs[..., :half_rot]
    second_half = inputs[..., half_rot:ROT]
    return jnp.concatenate([first_half * cosine - second_half * sine_part, second_half * cosine + first_half * sine_part, inputs[..., ROT:]], axis=-1)

def reference(hidden, group_qkv, mlp_branch, key_cache, paged_value_cache, cache_lengths, page_table, dense_weight, dense_bias, norm_gain, norm_bias, qkv_weight, qkv_bias):
    triples = group_qkv.astype(jnp.float32).reshape(TOKENS, HALF_HEADS, 3, HEAD_SIZE)
    row_ids = jnp.arange(TOKENS, dtype=jnp.int32)
    owner_id = row_ids // GROUP
    positions = cache_lengths[owner_id] + row_ids % GROUP
    queries = rotate_rows(triples[:, :, 0], positions).astype(jnp.bfloat16)
    new_keys = rotate_rows(triples[:, :, 1], positions).astype(jnp.bfloat16)
    new_values = group_qkv.reshape(TOKENS, HALF_HEADS, 3, HEAD_SIZE)[:, :, 2]
    slot_ids = page_table[owner_id, positions // PAGE_TOKENS]
    row_in_page = positions % PAGE_TOKENS
    key_out = key_cache.at[slot_ids, row_in_page].set(new_keys.reshape(TOKENS, HALF_HEADS * HEAD_SIZE))
    value_out = paged_value_cache.at[slot_ids, row_in_page].set(new_values.reshape(TOKENS, HALF_HEADS * HEAD_SIZE))
    score_scale = 1.0 / math.sqrt(HEAD_SIZE)

    def one_request(request_id):
        pages_of = page_table[request_id]
        kept_keys = key_out[pages_of].reshape(MAXP * PAGE_TOKENS, HALF_HEADS, HEAD_SIZE).astype(jnp.float32)
        kept_values = value_out[pages_of].reshape(MAXP * PAGE_TOKENS, HALF_HEADS, HEAD_SIZE).astype(jnp.float32)
        query_block = lax.dynamic_slice_in_dim(queries, request_id * GROUP, GROUP, 0).astype(jnp.float32)
        scores = jnp.einsum('chd,thd->hct', query_block, kept_keys) * score_scale
        length = cache_lengths[request_id]
        visible = jnp.arange(MAXP * PAGE_TOKENS, dtype=jnp.int32)[None, :] <= length + jnp.arange(GROUP, dtype=jnp.int32)[:, None]
        row_peak = lax.optimization_barrier(jnp.max(jnp.where(visible[None], scores, -1e+30), axis=2, keepdims=True))
        weights = jnp.where(visible[None], jnp.exp(scores - row_peak), 0.0)
        rounded = lax.optimization_barrier(weights.astype(jnp.bfloat16)).astype(jnp.float32)
        totals = lax.optimization_barrier(jnp.sum(weights, axis=2)).T
        weighted = jnp.einsum('hct,thd->chd', rounded, kept_values)
        return (weighted / totals[:, :, None]).reshape(GROUP, HALF_HEADS * HEAD_SIZE).astype(jnp.bfloat16)
    attention = lax.map(one_request, jnp.arange(REQS, dtype=jnp.int32)).reshape(TOKENS, HALF_HEADS * HEAD_SIZE)
    projected = jnp.dot(attention, dense_weight, preferred_element_type=jnp.float32)
    stream = (projected + dense_bias + hidden.astype(jnp.float32) + mlp_branch.astype(jnp.float32)).astype(jnp.bfloat16)
    widened = stream.astype(jnp.float32)
    row_mean = lax.optimization_barrier(jnp.sum(widened, axis=1)) / D
    variance = lax.optimization_barrier(jnp.sum(widened * widened, axis=1)) / D - row_mean * row_mean
    normed = ((widened - row_mean[:, None]) * lax.rsqrt(variance[:, None] + 1e-05) * norm_gain + norm_bias).astype(jnp.bfloat16)
    next_qkv = (jnp.dot(normed, qkv_weight, preferred_element_type=jnp.float32) + qkv_bias).astype(jnp.bfloat16)
    return (stream, next_qkv, key_out, value_out)
```

```python
import math

import jax
import jax.numpy as jnp
from jax import lax
from jax.experimental import pallas as pl
from jax.experimental.pallas import tpu as pltpu
from jax.sharding import PartitionSpec as P

D = 4096
HS = 128
ROT = 32
PT = 128
GROUP = 512
LH = 4
LW = LH * HS
SLOTS = 13
REQS = 8
MAXP = 36
TOK = 128
PIECES = LW + 32
COLS = D // 4
QW = 1536
NEG = -1e30
C2 = math.log2(math.e) / math.sqrt(HS)
F32 = jnp.float32
BF16 = jnp.bfloat16
VMEM = pltpu.VMEM
SMEM = pltpu.SMEM


def whole(space=VMEM):
    return pl.BlockSpec(memory_space=space)


def head_rows(h):
    return slice(h * HS, (h + 1) * HS)


def rotary_kernel(x_ref, cos_ref, sin_ref, q_ref, kv_ref):
    cosine = cos_ref[...]
    sine = sin_ref[...]
    half = ROT // 2
    for h in range(LH):
        for which in range(2):
            base = (3 * h + which) * HS
            turned = x_ref[:, base : base + HS].astype(F32).T
            a = turned[0:half]
            b = turned[half:ROT]
            done = jnp.concatenate(
                [a * cosine - b * sine, b * cosine + a * sine, turned[ROT:]], axis=0
            )
            if which == 0:
                q_ref[head_rows(h), :] = done.astype(BF16)
            else:
                kv_ref[:, head_rows(h)] = done.T.astype(BF16)
        base = (3 * h + 2) * HS
        kv_ref[:, LW + h * HS : LW + (h + 1) * HS] = x_ref[:, base : base + HS]


def rotary(group_qkv, cosine, sine):
    return pl.pallas_call(
        rotary_kernel,
        out_shape=(
            jax.ShapeDtypeStruct((LW, TOK), BF16),
            jax.ShapeDtypeStruct((TOK, 2 * LW), BF16),
        ),
        in_specs=[whole()] * 3,
        out_specs=(whole(), whole()),
        name="rotary",
    )(group_qkv, cosine, sine)


def split3(value):
    top = value.astype(BF16)
    rest = value - top.astype(F32)
    middle = rest.astype(BF16)
    low = (rest - middle.astype(F32)).astype(BF16)
    return top, middle, low


def stat_rows(stats):
    width = stats.shape[1]
    return jnp.concatenate(
        [piece.astype(F32) for piece in split3(stats)] + [jnp.zeros((8, width), F32)], axis=0
    ).astype(BF16)


def attention_kernel(with_fresh, info, lens, table, q_ref, k_own, v_own, k_other, v_other, *rest):
    if with_fresh:
        fresh_own, fresh_other, *rest = rest
    o_ref, kbuf, vbuf, sems, pages, qs, acc, stats = rest
    page = info[0]
    row = info[1]
    x = info[2]
    core = info[3]
    chip = lax.div(page, 2)

    def copies(n, local, k_src, v_src):
        return (
            pltpu.make_async_copy(k_src.at[local], kbuf.at[n], sems.at[n, 0]),
            pltpu.make_async_copy(v_src.at[local], vbuf.at[n], sems.at[n, 1]),
        )

    bounds = []
    count = jnp.int32(0)
    for part in range(2):
        request = 2 * row + part
        used = lax.div(lens[request] + (PT - 1), PT)

        def scan(g, n, request=request):
            slot = table[request, g]
            device = lax.div(slot, SLOTS)
            local = slot - device * SLOTS
            here = lax.div(device, 2) == chip

            @pl.when(here)
            def _():
                pages[n] = g

                @pl.when(device == page)
                def _():
                    for copy in copies(n, local, k_own, v_own):
                        copy.start()

                @pl.when(device != page)
                def _():
                    for copy in copies(n, local, k_other, v_other):
                        copy.start()

            return n + here.astype(jnp.int32)

        first = count
        count = lax.fori_loop(0, used, scan, count)
        bounds.append((first, count))

    key_row = lax.broadcasted_iota(jnp.int32, (PT, 2 * TOK), 0)
    lane = lax.broadcasted_iota(jnp.int32, (PT, 2 * TOK), 1)
    query_index = core * TOK + lane + jnp.where(lane >= TOK, TOK, 0)

    def absorb(key_of, value_of, mask, guard):
        old = stats[...]
        new_rows = []
        for h in range(LH):
            scores = jnp.dot(key_of(h), qs[h], preferred_element_type=F32)
            scores = jnp.where(mask, scores, NEG)
            old_peak = old[h : h + 1]
            peak = jnp.maximum(old_peak, jnp.max(scores, axis=0, keepdims=True))
            weights = jnp.exp2((scores - peak) * C2)
            if guard:
                weights = jnp.where(mask, weights, 0.0)
            decay = jnp.exp2((old_peak - peak) * C2)
            total = old[LH + h : LH + h + 1] * decay + jnp.sum(weights, axis=0, keepdims=True)
            acc[head_rows(h), :] = acc[head_rows(h), :] * decay + lax.dot_general(
                value_of(h), weights.astype(BF16), (((0,), (0,)), ((), ())),
                preferred_element_type=F32,
            )
            new_rows.append((peak, total))
        stats[...] = jnp.concatenate([r[0] for r in new_rows] + [r[1] for r in new_rows], axis=0)

    for part in range(2):
        request = 2 * row + part
        left = lax.bitwise_and(x - 2 * part, 3)
        right = lax.bitwise_and(x - 2 * part - 1, 3)
        for h in range(LH):
            qs[h] = jnp.concatenate(
                [q_ref[left, head_rows(h), :], q_ref[right, head_rows(h), :]], axis=1
            )
        acc[...] = jnp.zeros_like(acc)
        stats[...] = jnp.where(
            lax.broadcasted_iota(jnp.int32, (2 * LH, 2 * TOK), 0) < LH, NEG, 0.0
        )

        def step(n, carry, request=request):
            for copy in copies(n, 0, k_own, v_own):
                copy.wait()
            mask = key_row < lens[request] - pages[n] * PT
            absorb(
                lambda h: kbuf[n, :, head_rows(h)], lambda h: vbuf[n, :, head_rows(h)], mask, False
            )
            return carry

        first, last = bounds[part]
        lax.fori_loop(first, last, step, 0)
        if with_fresh:

            @pl.when(lax.div(x, 2) == part)
            def _():
                for source, index in ((fresh_own, core), (fresh_other, 1 - core)):
                    start = (2 * lax.bitwise_and(x, 1) + index) * TOK
                    absorb(
                        lambda h: source[:, head_rows(h)],
                        lambda h: source[:, LW + h * HS : LW + (h + 1) * HS],
                        start + key_row <= query_index,
                        True,
                    )

        tail = stat_rows(stats[...])
        for block, half in ((left, slice(0, TOK)), (right, slice(TOK, 2 * TOK))):
            for h in range(LH):
                o_ref[block, head_rows(h), :] = acc[head_rows(h), half].astype(BF16)
            o_ref[block, LW:PIECES, :] = tail[:, half]


def attend(info, lens, table, queries, caches, fresh):
    with_fresh = fresh is not None
    operands = [info, lens, table, queries, *caches] + (list(fresh) if with_fresh else [])
    specs = [whole(SMEM)] * 3 + [whole()] + [whole(pl.ANY)] * 4
    specs += [whole()] * 2 if with_fresh else []

    def body(*refs):
        attention_kernel(with_fresh, *refs)

    return pl.pallas_call(
        body,
        out_shape=jax.ShapeDtypeStruct((4, PIECES, TOK), BF16),
        in_specs=specs,
        out_specs=whole(),
        scratch_shapes=[
            VMEM((2 * SLOTS, PT, LW), BF16),
            VMEM((2 * SLOTS, PT, LW), BF16),
            pltpu.SemaphoreType.DMA((2 * SLOTS, 2)),
            SMEM((2 * SLOTS,), jnp.int32),
            VMEM((LH, HS, 2 * TOK), BF16),
            VMEM((LW, 2 * TOK), F32),
            VMEM((2 * LH, 2 * TOK), F32),
        ],
        compiler_params=pltpu.CompilerParams(vmem_limit_bytes=24 << 20),
        cost_estimate=pl.CostEstimate(
            flops=8 * 2 * 2 * PT * LW * 256, transcendentals=8 * PT * 4 * 256,
            bytes_accessed=3 << 20,
        ),
        name="attend_fresh" if with_fresh else "attend",
    )(*operands)


def join(parts):
    read = []
    for part in parts:
        tail = part[LW:PIECES].astype(F32)
        read.append(tail[0:8] + tail[8:16] + tail[16:24])
    peak = read[0][0:LH]
    for value in read[1:]:
        peak = jnp.maximum(peak, value[0:LH])
    factors = [jnp.exp2((value[0:LH] - peak) * C2) for value in read]
    total = sum(value[LH : 2 * LH] * factor for value, factor in zip(read, factors))
    weighted = [
        sum(
            part[head_rows(h)].astype(F32) * factor[h : h + 1]
            for part, factor in zip(parts, factors)
        )
        for h in range(LH)
    ]
    return peak, total, weighted


def join_rows_kernel(a_ref, b_ref, c_ref, d_ref, *outs):
    for block, out in enumerate(outs):
        parts = [ref.at[block] for ref in (a_ref, b_ref, c_ref, d_ref)]
        peak, total, weighted = join(parts)
        for h in range(LH):
            out[head_rows(h), :] = weighted[h].astype(BF16)
        out[LW:PIECES, :] = stat_rows(jnp.concatenate([peak, total], axis=0))


def join_last_kernel(a_ref, b_ref, c_ref, d_ref, out):
    _, total, weighted = join([a_ref, b_ref, c_ref, d_ref])
    inverse = 1.0 / total
    for h in range(LH):
        out[:, head_rows(h)] = (weighted[h] * inverse[h : h + 1]).T.astype(BF16)


def join_rows(parts):
    return pl.pallas_call(
        join_rows_kernel,
        out_shape=tuple(jax.ShapeDtypeStruct((PIECES, TOK), BF16) for _ in range(4)),
        in_specs=[whole()] * 4,
        out_specs=tuple(whole() for _ in range(4)),
        name="join_rows",
    )(*parts)


def join_last(parts):
    return pl.pallas_call(
        join_last_kernel,
        out_shape=jax.ShapeDtypeStruct((TOK, LW), BF16),
        in_specs=[whole()] * 4,
        out_specs=whole(),
        name="join_last",
    )(*parts)


def dense_kernel(*refs):
    attention = refs[0:4]
    weights = refs[4:8]
    bias, hidden, branch, out = refs[8:]
    total = bias[...] + hidden[...].astype(F32) + branch[...].astype(F32)
    product = jnp.dot(attention[0][...], weights[0][...], preferred_element_type=F32)
    for a, w in zip(attention[1:], weights[1:]):
        product = product + jnp.dot(a[...], w[...], preferred_element_type=F32)
    out[...] = (product + total).astype(BF16)


def dense(attention, weights, bias, hidden, branch):
    width = 512
    column = lambda rows: pl.BlockSpec((rows, width), lambda i: (0, i))
    return pl.pallas_call(
        dense_kernel,
        grid=(COLS // width,),
        out_shape=jax.ShapeDtypeStruct((TOK, COLS), BF16),
        in_specs=[pl.BlockSpec((TOK, LW), lambda i: (0, 0))] * 4
        + [column(LW)] * 4
        + [column(1), column(TOK), column(TOK)],
        out_specs=column(TOK),
        compiler_params=pltpu.CompilerParams(vmem_limit_bytes=24 << 20),
        name="dense",
    )(*attention, *weights, bias, hidden, branch)


WROWS = 512


def qkv_kernel(info, x0, x1, x2, x3, gain, shift, weight, bias, out, wbuf, sems):
    head = info[4]
    per = COLS // WROWS
    chunks = []
    for s in range(4):
        origin = lax.bitwise_and(head - s, 3)
        for j in range(per):
            start = pl.multiple_of(origin * COLS + j * WROWS, WROWS)
            n = s * per + j
            chunks.append(
                pltpu.make_async_copy(weight.at[pl.ds(start, WROWS), :], wbuf.at[n], sems.at[n])
            )
    for copy in chunks:
        copy.start()
    blocks = (x0, x1, x2, x3)
    total = 0.0
    square = 0.0
    for block in blocks:
        value = block[...].astype(F32)
        total = total + jnp.sum(value, axis=1, keepdims=True)
        square = square + jnp.sum(value * value, axis=1, keepdims=True)
    mean = total / D
    variance = square / D - mean * mean
    scale = lax.rsqrt(variance + 1e-05)
    result = bias[...] + jnp.zeros((TOK, QW), F32)
    for s, block in enumerate(blocks):
        origin = lax.bitwise_and(head - s, 3)
        normed = (block[...].astype(F32) - mean) * scale * gain[pl.ds(origin, 1), :]
        normed = (normed + shift[pl.ds(origin, 1), :]).astype(BF16)
        for j in range(per):
            n = s * per + j
            chunks[n].wait()
            result = result + jnp.dot(
                normed[:, j * WROWS : (j + 1) * WROWS], wbuf[n], preferred_element_type=F32
            )
    out[...] = result.astype(BF16)


def project_qkv(info, blocks, gain, shift, weight, bias):
    return pl.pallas_call(
        qkv_kernel,
        out_shape=jax.ShapeDtypeStruct((TOK, QW), BF16),
        in_specs=[whole(SMEM)] + [whole()] * 6 + [whole(pl.ANY), whole()],
        out_specs=whole(),
        scratch_shapes=[
            VMEM((D // WROWS, WROWS, QW), BF16),
            pltpu.SemaphoreType.DMA((D // WROWS,)),
        ],
        compiler_params=pltpu.CompilerParams(vmem_limit_bytes=32 << 20),
        name="project_qkv",
    )(info, *blocks, gain, shift, weight, bias)


WINDOW = 256
FRESH_PAGES = GROUP // PT + 1


def patch_kernel(
    info, lens, table, new_ref, k_in, v_in, k_out, v_out, src, kbuf, vbuf, sems, slots, shifts, starts
):
    page = info[0]

    def loads(n, local, start):
        return (
            pltpu.make_async_copy(new_ref.at[pl.ds(start, WINDOW), :], src.at[n], sems.at[n, 0]),
            pltpu.make_async_copy(k_in.at[local], kbuf.at[n], sems.at[n, 1]),
            pltpu.make_async_copy(v_in.at[local], vbuf.at[n], sems.at[n, 2]),
        )

    def stores(n, local):
        return (
            pltpu.make_async_copy(kbuf.at[n], k_out.at[local], sems.at[n, 3]),
            pltpu.make_async_copy(vbuf.at[n], v_out.at[local], sems.at[n, 4]),
        )

    def scan_request(request, count):
        length = lens[request]
        first = lax.div(length, PT)
        last = lax.div(length + (GROUP - 1), PT)

        def scan(g, n):
            slot = table[request, g]
            here = lax.div(slot, SLOTS) == page

            @pl.when(here)
            def _():
                local = slot - page * SLOTS
                offset = g * PT - length
                exact = request * GROUP + jnp.maximum(offset, 0)
                start = jnp.minimum(lax.div(exact, 16) * 16, REQS * GROUP - WINDOW)
                start = pl.multiple_of(start, 16)
                slots[n] = local
                shifts[n] = request * GROUP + offset - start
                starts[n] = offset
                for copy in loads(n, local, start):
                    copy.start()

            return n + here.astype(jnp.int32)

        return lax.fori_loop(first, last + 1, scan, count)

    count = lax.fori_loop(0, REQS, scan_request, jnp.int32(0))
    pick_row = lax.broadcasted_iota(jnp.int32, (PT, WINDOW), 0)
    pick_col = lax.broadcasted_iota(jnp.int32, (PT, WINDOW), 1)
    token = lax.broadcasted_iota(jnp.int32, (PT, LW), 0)

    def update(n, carry):
        for copy in loads(n, 0, 0):
            copy.wait()
        pick = jnp.where(pick_col == pick_row + shifts[n], 1.0, 0.0).astype(BF16)
        index = token + starts[n]
        fresh = (index >= 0) & (index < GROUP)
        for buf, cols in ((kbuf, slice(0, LW)), (vbuf, slice(LW, 2 * LW))):
            moved = jnp.dot(pick, src[n, :, cols], preferred_element_type=F32)
            buf[n] = jnp.where(fresh, moved, buf[n].astype(F32)).astype(BF16)
        for copy in stores(n, slots[n]):
            copy.start()
        return carry

    def finish(n, carry):
        for copy in stores(n, 0):
            copy.wait()
        return carry

    lax.fori_loop(0, count, update, 0)
    lax.fori_loop(0, count, finish, 0)


def patch(info, lens, table, new, key_cache, value_cache):
    shape = jax.ShapeDtypeStruct(key_cache.shape, BF16)
    return pl.pallas_call(
        patch_kernel,
        out_shape=(shape, shape),
        in_specs=[whole(SMEM)] * 3 + [whole(pl.ANY)] * 3,
        out_specs=(whole(pl.ANY), whole(pl.ANY)),
        scratch_shapes=[
            VMEM((SLOTS, WINDOW, 2 * LW), BF16),
            VMEM((SLOTS, PT, LW), BF16),
            VMEM((SLOTS, PT, LW), BF16),
            pltpu.SemaphoreType.DMA((SLOTS, 5)),
            SMEM((SLOTS,), jnp.int32),
            SMEM((SLOTS,), jnp.int32),
            SMEM((SLOTS,), jnp.int32),
        ],
        input_output_aliases={4: 0, 5: 1},
        compiler_params=pltpu.CompilerParams(vmem_limit_bytes=32 << 20),
        name="patch",
    )(info, lens, table, new, key_cache, value_cache)


def plane_shift(dy, dx):
    return [
        (y * 8 + x * 2 + c, ((y + dy) % 4) * 8 + ((x + dx) % 4) * 2 + c)
        for y in range(4)
        for x in range(4)
        for c in range(2)
    ]


CORES = [(p, p ^ 1) for p in range(32)]


def head_shift(s):
    return [(i, (i + s) % 4) for i in range(4)]


def on_device(
    hidden,
    group_qkv,
    mlp_branch,
    key_cache,
    paged_value_cache,
    cache_lengths,
    page_table,
    dense_weight,
    dense_bias,
    norm_gain,
    norm_bias,
    qkv_weight,
    qkv_bias,
):
    page = lax.axis_index("page").astype(jnp.int32)
    head = lax.axis_index("head").astype(jnp.int32)
    y = page // 8
    x = (page // 2) % 4
    core = page % 2

    def info_for(row):
        return jnp.stack([page, row, x, core, head])

    length = lax.dynamic_index_in_dim(cache_lengths, page // 4, 0, keepdims=False)
    positions = length + (page % 4) * TOK + jnp.arange(TOK, dtype=jnp.int32)
    inverse = 1.0 / 10000.0 ** (jnp.arange(0, ROT, 2, dtype=F32) / ROT)
    angles = positions.astype(F32)[None, :] * inverse[:, None]
    queries, fresh = rotary(group_qkv, jnp.cos(angles), jnp.sin(angles))

    row_queries = [queries] + [
        lax.ppermute(queries, "page", plane_shift(0, s)) for s in range(1, 4)
    ]
    row_queries = jnp.stack(row_queries, axis=0)
    all_queries = [row_queries] + [
        lax.ppermute(row_queries, "page", plane_shift(s, 0)) for s in range(1, 4)
    ]

    other_keys = lax.ppermute(key_cache, "page", CORES)
    other_values = lax.ppermute(paged_value_cache, "page", CORES)
    other_fresh = lax.ppermute(fresh, "page", CORES)
    caches = (key_cache, paged_value_cache, other_keys, other_values)

    new_rows = lax.all_gather(fresh, "page", axis=0, tiled=True)

    weights = [
        lax.dynamic_slice_in_dim(dense_weight, ((head + s) % 4) * COLS, COLS, 1) for s in range(4)
    ]
    weights = weights[:1] + [
        lax.ppermute(weights[s], "head", head_shift(s)) for s in range(1, 4)
    ]

    partials = []
    for s in range(4):
        part = attend(
            info_for((y - s) % 4),
            cache_lengths,
            page_table,
            all_queries[s],
            caches,
            (fresh, other_fresh) if s == 0 else None,
        )
        partials.append(part if s == 0 else lax.ppermute(part, "page", plane_shift(-s, 0)))
    blocks = join_rows(partials)
    blocks = [blocks[0]] + [
        lax.ppermute(blocks[s], "page", plane_shift(0, -s)) for s in range(1, 4)
    ]
    attention = join_last(blocks)

    attention = [attention] + [
        lax.ppermute(attention, "head", head_shift(s)) for s in range(1, 4)
    ]
    share_bias = lax.dynamic_slice_in_dim(dense_bias, head * COLS, COLS, 0)[None, :]
    new_hidden = dense(attention, weights, share_bias, hidden, mlp_branch)

    streams = [new_hidden] + [
        lax.ppermute(new_hidden, "head", head_shift(s)) for s in range(1, 4)
    ]
    next_qkv = project_qkv(
        info_for(y),
        streams,
        norm_gain.reshape(4, COLS),
        norm_bias.reshape(4, COLS),
        qkv_weight,
        qkv_bias[None, :],
    )

    key_out, value_out = patch(
        info_for(y), cache_lengths, page_table, new_rows, key_cache, paged_value_cache
    )
    return (new_hidden, next_qkv, key_out, value_out)


def solution(mesh):
    in_specs = (
        P("page", "head"),
        P("page", "head"),
        P("page", "head"),
        P("page", None, "head"),
        P("page", None, "head"),
        P(),
        P(),
        P("head", None),
        P(),
        P(),
        P(),
        P(None, "head"),
        P("head"),
    )
    out_specs = (
        P("page", "head"),
        P("page", "head"),
        P("page", None, "head"),
        P("page", None, "head"),
    )
    return jax.shard_map(
        on_device, mesh=mesh, in_specs=in_specs, out_specs=out_specs, check_vma=False
    )
```

```python
import math

import jax
import jax.numpy as jnp
from jax import lax
from jax.experimental import pallas as pl
from jax.experimental.pallas import tpu as pltpu
from jax.sharding import Mesh
from jax.sharding import PartitionSpec as P

D = 4096
HS = 128
ROT = 32
PT = 128
GROUP = 512
LH = 4
LW = LH * HS
SLOTS = 13
REQS = 8
MAXP = 36
TOK = 128
PIECES = LW + 32
COLS = D // 4
QW = 1536
NEG = -1e30
C2 = math.log2(math.e) / math.sqrt(HS)
F32 = jnp.float32
BF16 = jnp.bfloat16
VMEM = pltpu.VMEM
HBM = pltpu.HBM
SMEM = pltpu.SMEM


def whole(space=VMEM):
    return pl.BlockSpec(memory_space=space)


def limit(mib):
    return pltpu.CompilerParams(vmem_limit_bytes=mib << 20)


def head_rows(h):
    return slice(h * HS, (h + 1) * HS)


def rotary_kernel(info, lens, x_ref, rate_ref, q_ref, kv_ref):
    half = ROT // 2
    page = info[0]
    first = lens[lax.div(page, 4)] + lax.rem(page, 4) * TOK
    lane = lax.broadcasted_iota(jnp.int32, (half, TOK), 1)
    angles = (first + lane).astype(F32) * rate_ref[...]
    cosine = jnp.cos(angles)
    sine = jnp.sin(angles)
    for h in range(LH):
        for which in range(2):
            base = (3 * h + which) * HS
            turned = x_ref[:, base : base + HS].astype(F32).T
            a = turned[0:half]
            b = turned[half:ROT]
            done = jnp.concatenate(
                [a * cosine - b * sine, b * cosine + a * sine, turned[ROT:]], axis=0
            )
            if which == 0:
                q_ref[head_rows(h), :] = done.astype(BF16)
            else:
                kv_ref[:, head_rows(h)] = done.T.astype(BF16)
        base = (3 * h + 2) * HS
        kv_ref[:, LW + h * HS : LW + (h + 1) * HS] = x_ref[:, base : base + HS]


def rotary(info, lens, group_qkv, rates):
    return pl.pallas_call(
        rotary_kernel,
        out_shape=(
            jax.ShapeDtypeStruct((LW, TOK), BF16),
            jax.ShapeDtypeStruct((TOK, 2 * LW), BF16),
        ),
        in_specs=[whole(SMEM)] * 2 + [whole()] * 2,
        out_specs=(whole(), whole()),
        compiler_params=limit(2),
        name="rotary",
    )(info, lens, group_qkv, rates)


def stack_kernel(*refs):
    for i, ref in enumerate(refs[:-1]):
        refs[-1][i] = ref[...]


def stack(parts):
    return pl.pallas_call(
        stack_kernel,
        out_shape=jax.ShapeDtypeStruct((len(parts),) + parts[0].shape, parts[0].dtype),
        in_specs=[whole()] * len(parts),
        out_specs=whole(),
        compiler_params=limit(6),
        name="stack",
    )(*parts)


LIST = 32


def pool_kernel(info, lens, table, k_other, v_other, keys, values, codes, counts, sems):
    page = info[0]
    chip = lax.div(page, 2)
    copies = [
        pltpu.make_async_copy(src.at[i], dst.at[i], sems.at[n, i])
        for n, (src, dst) in enumerate(((k_other, keys), (v_other, values)))
        for i in range(SLOTS)
    ]
    for copy in copies:
        copy.start()

    def scan_request(request, carry):
        def scan(g, n):
            slot = table[request, g]
            device = lax.div(slot, SLOTS)
            here = lax.div(device, 2) == chip

            @pl.when(here)
            def _():
                local = slot - device * SLOTS
                local = jnp.where(device == page, local, local + SLOTS)
                codes[request, n] = g * LIST + local

            return n + here.astype(jnp.int32)

        used = lax.div(lens[request] + (PT - 1), PT)
        counts[request] = lax.fori_loop(0, used, scan, jnp.int32(0))
        return carry

    lax.fori_loop(0, REQS, scan_request, 0)
    for copy in copies:
        copy.wait()


def pool(info, lens, table, k_other, v_other):
    shape = jax.ShapeDtypeStruct(k_other.shape, BF16)
    return pl.pallas_call(
        pool_kernel,
        out_shape=(
            shape,
            shape,
            jax.ShapeDtypeStruct((REQS, LIST), jnp.int32),
            jax.ShapeDtypeStruct((REQS,), jnp.int32),
        ),
        in_specs=[whole(SMEM)] * 3 + [whole(HBM)] * 2,
        out_specs=(whole(), whole(), whole(SMEM), whole(SMEM)),
        scratch_shapes=[pltpu.SemaphoreType.DMA((2, SLOTS))],
        compiler_params=limit(8),
        name="pool",
    )(info, lens, table, k_other, v_other)


PARTS = 32


def load_kernel(src, dst, sems):
    rows = src.shape[0] // PARTS
    copies = [
        pltpu.make_async_copy(
            src.at[pl.ds(i * rows, rows)], dst.at[pl.ds(i * rows, rows)], sems.at[i]
        )
        for i in range(PARTS)
    ]
    for copy in copies:
        copy.start()
    for copy in copies:
        copy.wait()


def load(array):
    return pl.pallas_call(
        load_kernel,
        out_shape=jax.ShapeDtypeStruct(array.shape, array.dtype),
        in_specs=[whole(HBM)],
        out_specs=whole(),
        scratch_shapes=[pltpu.SemaphoreType.DMA((PARTS,))],
        compiler_params=limit(40),
        name="load",
    )(array)


def split3(value):
    top = value.astype(BF16)
    rest = value - top.astype(F32)
    middle = rest.astype(BF16)
    low = (rest - middle.astype(F32)).astype(BF16)
    return top, middle, low


def stat_rows(stats):
    width = stats.shape[1]
    return jnp.concatenate(
        [piece.astype(F32) for piece in split3(stats)] + [jnp.zeros((8, width), F32)], axis=0
    ).astype(BF16)


def attention_kernel(
    step, info, lens, codes, counts, q_ref, k_own, v_own, k_other, v_other, *rest
):
    if step != 2:
        fresh_own, fresh_other, *rest = rest
    o_ref, acc, stats = rest
    y = info[1]
    x = info[2]
    core = info[3]
    key_row = lax.broadcasted_iota(jnp.int32, (2 * PT, TOK), 0)
    lane = lax.broadcasted_iota(jnp.int32, (2 * PT, TOK), 1)

    def block_loop(block, carry):
        row = lax.bitwise_and(y - jnp.where(core == 0, step, block), 3)
        column = lax.bitwise_and(x - jnp.where(core == 0, block, step), 3)
        request = 2 * row + lax.div(column, 2)

        def absorb(key_of, value_of, mask, guard):
            old = stats[...]
            scores = [
                jnp.where(
                    mask,
                    jnp.dot(key_of(h), q_ref[block, head_rows(h), :], preferred_element_type=F32),
                    NEG,
                )
                for h in range(LH)
            ]
            peaks = [
                jnp.maximum(old[h : h + 1], jnp.max(scores[h], axis=0, keepdims=True))
                for h in range(LH)
            ]
            weights = [jnp.exp2((scores[h] - peaks[h]) * C2) for h in range(LH)]
            if guard:
                weights = [jnp.where(mask, w, 0.0) for w in weights]
            decays = [jnp.exp2((old[h : h + 1] - peaks[h]) * C2) for h in range(LH)]
            totals = [
                old[LH + h : LH + h + 1] * decays[h] + jnp.sum(weights[h], axis=0, keepdims=True)
                for h in range(LH)
            ]
            stats[...] = jnp.concatenate(peaks + totals, axis=0)
            added = [
                lax.dot_general(
                    value_of(h), weights[h].astype(BF16), (((0,), (0,)), ((), ())),
                    preferred_element_type=F32,
                )
                for h in range(LH)
            ]
            for h in range(LH):
                acc[head_rows(h), :] = acc[head_rows(h), :] * decays[h] + added[h]

        acc[...] = jnp.zeros_like(acc)
        stats[...] = jnp.where(lax.broadcasted_iota(jnp.int32, (2 * LH, TOK), 0) < LH, NEG, 0.0)
        count = counts[request]

        def pages_step(i, inner):
            full = 2 * i + 1 < count
            first = codes[request, 2 * i]
            second = codes[request, jnp.where(full, 2 * i + 1, 2 * i)]
            lower = lens[request] - lax.div(first, LIST) * PT
            upper = jnp.where(full, lens[request] - lax.div(second, LIST) * PT, 0) + PT
            mask = key_row < jnp.where(key_row < PT, lower, upper)

            def page_rows(own, other, code, h):
                slot = lax.rem(code, LIST)
                mine = slot < SLOTS
                local = jnp.where(mine, slot, slot - SLOTS)
                return jnp.where(
                    mine, own[local, :, head_rows(h)], other[local, :, head_rows(h)]
                )

            def pair(own, other, h):
                return jnp.concatenate(
                    [page_rows(own, other, first, h), page_rows(own, other, second, h)], axis=0
                )

            absorb(
                lambda h: pair(k_own, k_other, h), lambda h: pair(v_own, v_other, h), mask, False
            )
            return inner

        lax.fori_loop(0, lax.div(count + 1, 2), pages_step, 0)
        if step != 2:

            @pl.when(request == 2 * y + lax.div(x, 2))
            def _():
                pair = lambda cols: jnp.concatenate(
                    [fresh_own[:, cols], fresh_other[:, cols]], axis=0
                )
                token = 2 * lax.bitwise_and(x, 1) * TOK + jnp.where(
                    key_row < PT, key_row + core * TOK, key_row - core * TOK
                )
                query = (2 * lax.bitwise_and(column, 1) + core) * TOK + lane
                absorb(
                    lambda h: pair(head_rows(h)),
                    lambda h: pair(slice(LW + h * HS, LW + (h + 1) * HS)),
                    token <= query,
                    True,
                )

        for h in range(LH):
            o_ref[block, head_rows(h), :] = acc[head_rows(h), :].astype(BF16)
        o_ref[block, LW:PIECES, :] = stat_rows(stats[...])
        return carry

    lax.fori_loop(0, 4, block_loop, 0)


def attend(step, info, lens, lists, queries, caches, fresh):
    operands = [info, lens, *lists, queries, *caches] + ([] if step == 2 else list(fresh))
    specs = [whole(SMEM)] * 4 + [whole()] * (5 if step == 2 else 7)

    def body(*refs):
        attention_kernel(step, *refs)

    return pl.pallas_call(
        body,
        out_shape=jax.ShapeDtypeStruct((4, PIECES, TOK), BF16),
        in_specs=specs,
        out_specs=whole(),
        scratch_shapes=[VMEM((LW, TOK), F32), VMEM((2 * LH, TOK), F32)],
        compiler_params=limit(12),
        cost_estimate=pl.CostEstimate(flops=0, transcendentals=0, bytes_accessed=0),
        name="attend%d" % step,
    )(*operands)


def join(parts):
    read = []
    for part in parts:
        tail = part[LW:PIECES].astype(F32)
        read.append(tail[0:8] + tail[8:16] + tail[16:24])
    peak = read[0][0:LH]
    for value in read[1:]:
        peak = jnp.maximum(peak, value[0:LH])
    factors = [jnp.exp2((value[0:LH] - peak) * C2) for value in read]
    total = sum(value[LH : 2 * LH] * factor for value, factor in zip(read, factors))
    weighted = [
        sum(
            part[head_rows(h)].astype(F32) * factor[h : h + 1]
            for part, factor in zip(parts, factors)
        )
        for h in range(LH)
    ]
    return peak, total, weighted


def join_rows_kernel(a_ref, b_ref, c_ref, d_ref, *outs):
    for block, out in enumerate(outs):
        parts = [ref.at[block] for ref in (a_ref, b_ref, c_ref, d_ref)]
        peak, total, weighted = join(parts)
        for h in range(LH):
            out[head_rows(h), :] = weighted[h].astype(BF16)
        out[LW:PIECES, :] = stat_rows(jnp.concatenate([peak, total], axis=0))


def join_last_kernel(a_ref, b_ref, c_ref, d_ref, out):
    _, total, weighted = join([a_ref, b_ref, c_ref, d_ref])
    inverse = 1.0 / total
    for h in range(LH):
        out[:, head_rows(h)] = (weighted[h] * inverse[h : h + 1]).T.astype(BF16)


def join_rows(parts):
    return pl.pallas_call(
        join_rows_kernel,
        out_shape=tuple(jax.ShapeDtypeStruct((PIECES, TOK), BF16) for _ in range(4)),
        in_specs=[whole()] * 4,
        out_specs=tuple(whole() for _ in range(4)),
        compiler_params=limit(8),
        name="join_rows",
    )(*parts)


def join_last(parts):
    return pl.pallas_call(
        join_last_kernel,
        out_shape=jax.ShapeDtypeStruct((TOK, LW), BF16),
        in_specs=[whole()] * 4,
        out_specs=whole(),
        compiler_params=limit(4),
        name="join_last",
    )(*parts)


def dense_kernel(info, attention, weight, bias, hidden, branch, own, *outs):
    head = info[4]
    base = pl.ds(pl.multiple_of(head * COLS, COLS), COLS)
    for s in range(4):
        target = lax.bitwise_and(head + s, 3)
        cols = pl.ds(pl.multiple_of(target * COLS, COLS), COLS)
        product = jnp.dot(attention[...], weight[:, cols], preferred_element_type=F32)
        if s == 0:
            rest = bias[base].reshape(1, COLS) + hidden[...].astype(F32) + branch[...].astype(F32)
            own[...] = product + rest
        else:
            outs[s - 1][...] = product.astype(BF16)


def dense(info, attention, weight, bias, hidden, branch):
    shape = jax.ShapeDtypeStruct((TOK, COLS), BF16)
    return pl.pallas_call(
        dense_kernel,
        out_shape=(jax.ShapeDtypeStruct((TOK, COLS), F32), shape, shape, shape),
        in_specs=[whole(SMEM)] + [whole()] * 5,
        out_specs=(whole(),) * 4,
        compiler_params=limit(10),
        name="dense",
    )(info, attention, weight, bias, hidden, branch)


def join_shares_kernel(own, a, b, c, out):
    out[...] = (
        own[...] + (a[...].astype(F32) + b[...].astype(F32) + c[...].astype(F32))
    ).astype(BF16)


def join_shares(parts):
    return pl.pallas_call(
        join_shares_kernel,
        out_shape=jax.ShapeDtypeStruct((TOK, COLS), BF16),
        in_specs=[whole()] * 4,
        out_specs=whole(),
        compiler_params=limit(4),
        name="join_shares",
    )(*parts)


def qkv_kernel(info, x0, x1, x2, x3, gain, shift, weight, bias, out):
    head = info[4]
    blocks = (x0, x1, x2, x3)
    total = 0.0
    square = 0.0
    for block in blocks:
        value = block[...].astype(F32)
        total = total + jnp.sum(value, axis=1, keepdims=True)
        square = square + jnp.sum(value * value, axis=1, keepdims=True)
    mean = total / D
    variance = square / D - mean * mean
    scale = lax.rsqrt(variance + 1e-05)
    result = bias[...].reshape(1, QW) + jnp.zeros((TOK, QW), F32)
    for s, block in enumerate(blocks):
        origin = lax.bitwise_and(head - s, 3)
        rows = pl.ds(pl.multiple_of(origin * COLS, COLS), COLS)
        normed = (block[...].astype(F32) - mean) * scale * gain[rows].reshape(1, COLS)
        normed = (normed + shift[rows].reshape(1, COLS)).astype(BF16)
        result = result + jnp.dot(normed, weight[rows, :], preferred_element_type=F32)
    out[...] = result.astype(BF16)


def project_qkv(info, blocks, gain, shift, weight, bias):
    return pl.pallas_call(
        qkv_kernel,
        out_shape=jax.ShapeDtypeStruct((TOK, QW), BF16),
        in_specs=[whole(SMEM)] + [whole()] * 8,
        out_specs=whole(),
        compiler_params=limit(20),
        name="project_qkv",
    )(info, *blocks, gain, shift, weight, bias)


WINDOW = 2 * TOK


def patch_kernel(info, lens, table, *refs):
    news = refs[0:2]
    k_in, v_in, k_out, v_out, src, kbuf, vbuf, sems, bulk, slots, offsets = refs[2:]
    page = info[0]
    core = info[3]
    whole_copies = (
        pltpu.make_async_copy(k_in, k_out, bulk.at[0]),
        pltpu.make_async_copy(v_in, v_out, bulk.at[1]),
    )
    for copy in whole_copies:
        copy.start()

    def source(n, half, ref, block):
        return pltpu.make_async_copy(
            ref.at[block], src.at[n, pl.ds(half * TOK, TOK), :], sems.at[n, half]
        )

    def loads(n, local):
        return (
            pltpu.make_async_copy(k_in.at[local], kbuf.at[n], sems.at[n, 2]),
            pltpu.make_async_copy(v_in.at[local], vbuf.at[n], sems.at[n, 3]),
        )

    def stores(n, local):
        return (
            pltpu.make_async_copy(kbuf.at[n], k_out.at[local], sems.at[n, 4]),
            pltpu.make_async_copy(vbuf.at[n], v_out.at[local], sems.at[n, 5]),
        )

    def scan_request(request, count):
        length = lens[request]
        first = lax.div(length, PT)
        last = lax.div(length + (GROUP - 1), PT)

        def scan(g, n):
            slot = table[request, g]
            here = lax.div(slot, SLOTS) == page

            @pl.when(here)
            def _():
                local = slot - page * SLOTS
                offset = g * PT - length
                lower = lax.div(offset + PT, PT) - 1
                slots[n] = local
                offsets[n] = offset
                for copy in loads(n, local):
                    copy.start()
                for half in range(2):
                    block = jnp.clip(lower + half, 0, 3)
                    chip = 2 * request + lax.div(block, 2)
                    mine = lax.rem(block, 2) == core

                    @pl.when(mine)
                    def _(half=half, chip=chip):
                        source(n, half, news[0], chip).start()

                    @pl.when(jnp.logical_not(mine))
                    def _(half=half, chip=chip):
                        source(n, half, news[1], chip).start()

            return n + here.astype(jnp.int32)

        return lax.fori_loop(first, last + 1, scan, count)

    count = lax.fori_loop(0, REQS, scan_request, jnp.int32(0))
    pick_row = lax.broadcasted_iota(jnp.int32, (PT, WINDOW), 0)
    pick_col = lax.broadcasted_iota(jnp.int32, (PT, WINDOW), 1)
    token = lax.broadcasted_iota(jnp.int32, (PT, LW), 0)

    def update(n, carry):
        for half in range(2):
            source(n, half, news[0], 0).wait()
        for copy in loads(n, 0):
            copy.wait()
        offset = offsets[n]
        base = (lax.div(offset + PT, PT) - 1) * PT
        pick = jnp.where(pick_col == pick_row + (offset - base), 1.0, 0.0).astype(BF16)
        index = token + offset
        fresh = (index >= 0) & (index < GROUP)
        for buf, cols in ((kbuf, slice(0, LW)), (vbuf, slice(LW, 2 * LW))):
            moved = jnp.dot(pick, src[n, :, cols], preferred_element_type=F32)
            buf[n] = jnp.where(fresh, moved, buf[n].astype(F32)).astype(BF16)
        return carry

    def put(n, carry):
        for copy in stores(n, slots[n]):
            copy.start()
        return carry

    def finish(n, carry):
        for copy in stores(n, 0):
            copy.wait()
        return carry

    lax.fori_loop(0, count, update, 0)
    for copy in whole_copies:
        copy.wait()
    lax.fori_loop(0, count, put, 0)
    lax.fori_loop(0, count, finish, 0)


def patch(info, lens, table, news, key_cache, value_cache):
    shape = jax.ShapeDtypeStruct(key_cache.shape, BF16)
    return pl.pallas_call(
        patch_kernel,
        out_shape=(shape, shape),
        in_specs=[whole(SMEM)] * 3 + [whole(HBM)] * 4,
        out_specs=(whole(HBM), whole(HBM)),
        scratch_shapes=[
            VMEM((SLOTS, WINDOW, 2 * LW), BF16),
            VMEM((SLOTS, PT, LW), BF16),
            VMEM((SLOTS, PT, LW), BF16),
            pltpu.SemaphoreType.DMA((SLOTS, 6)),
            pltpu.SemaphoreType.DMA((2,)),
            SMEM((SLOTS,), jnp.int32),
            SMEM((SLOTS,), jnp.int32),
        ],
        compiler_params=pltpu.CompilerParams(vmem_limit_bytes=20 << 20),
        name="patch",
    )(info, lens, table, *news, key_cache, value_cache)


def shift(s):
    return [(i, (i + s) % 4) for i in range(4)]


PLANE = ("y", "x", "core")
CORES = [(0, 1), (1, 0)]


def plane_shift(s, stage):
    pairs = []
    for y in range(4):
        for x in range(4):
            for c in range(2):
                along_x = (c == 0) == (stage == 0)
                to_y, to_x = (y, (x + s) % 4) if along_x else ((y + s) % 4, x)
                pairs.append((y * 8 + x * 2 + c, to_y * 8 + to_x * 2 + c))
    return pairs


def send(array, s, stage):
    return lax.ppermute(array, PLANE, plane_shift(s, stage))


def on_device(
    hidden,
    group_qkv,
    mlp_branch,
    key_cache,
    paged_value_cache,
    cache_lengths,
    page_table,
    dense_weight,
    dense_bias,
    norm_gain,
    norm_bias,
    qkv_weight,
    qkv_bias,
):
    y = lax.axis_index("y").astype(jnp.int32)
    x = lax.axis_index("x").astype(jnp.int32)
    core = lax.axis_index("core").astype(jnp.int32)
    head = lax.axis_index("head").astype(jnp.int32)
    page = 8 * y + 2 * x + core

    info = jnp.stack([page, y, x, core, head])

    inverse = 1.0 / 10000.0 ** (jnp.arange(0, ROT, 2, dtype=F32) / ROT)
    rates = jnp.broadcast_to(inverse[:, None], (ROT // 2, TOK))
    queries, fresh = rotary(info, cache_lengths, group_qkv, rates)

    gathered = lax.all_gather(fresh, ("y", "x"), axis=0)
    other_keys = lax.ppermute(key_cache, "core", CORES)
    other_values = lax.ppermute(paged_value_cache, "core", CORES)
    other_fresh = lax.ppermute(fresh, "core", CORES)
    near = [queries] + [send(queries, s, 0) for s in range(1, 4)]
    near = stack(near)
    all_queries = [near] + [send(near, s, 1) for s in range(1, 4)]

    pool_keys, pool_values, codes, counts = pool(
        info, cache_lengths, page_table, other_keys, other_values
    )
    caches = (key_cache, paged_value_cache, pool_keys, pool_values)

    partials = [None] * 4
    last = None
    for s in (0, 1, 3, 2):
        wanted = all_queries[s]
        if last is not None:
            wanted, last = lax.optimization_barrier((wanted, last))
        part = attend(
            s, info, cache_lengths, (codes, counts), wanted, caches, (fresh, other_fresh)
        )
        if last is not None:
            partials[before] = last if before == 0 else send(last, -before, 1)
        last, before = part, s
    partials[before] = send(last, -before, 1)
    blocks = join_rows(partials)
    blocks, gathered = lax.optimization_barrier((blocks, gathered))
    news = (gathered, lax.ppermute(gathered, "core", CORES))
    blocks = [blocks[0]] + [send(blocks[s], -s, 0) for s in range(1, 4)]
    attention = join_last(blocks)

    shares = dense(info, attention, dense_weight, dense_bias, hidden, mlp_branch)
    shares = [shares[0]] + [lax.ppermute(shares[s], "head", shift(s)) for s in range(1, 4)]
    new_hidden = join_shares(shares)

    streams = [new_hidden] + [lax.ppermute(new_hidden, "head", shift(s)) for s in range(1, 4)]
    late_weight, _ = lax.optimization_barrier((qkv_weight, new_hidden))
    next_qkv = project_qkv(
        info, streams, norm_gain, norm_bias, load(late_weight), qkv_bias
    )

    key_out, value_out = patch(
        info, cache_lengths, page_table, news, key_cache, paged_value_cache
    )
    return (new_hidden, next_qkv, key_out, value_out)


def solution(mesh):
    plane = PLANE
    fine = Mesh(mesh.devices.reshape(4, 4, 4, 2), ("head",) + plane)
    in_specs = (
        P(plane, "head"),
        P(plane, "head"),
        P(plane, "head"),
        P(plane, None, "head"),
        P(plane, None, "head"),
        P(),
        P(),
        P("head", None),
        P(),
        P(),
        P(),
        P(None, "head"),
        P("head"),
    )
    out_specs = (
        P(plane, "head"),
        P(plane, "head"),
        P(plane, None, "head"),
        P(plane, None, "head"),
    )
    return jax.shard_map(
        on_device, mesh=fine, in_specs=in_specs, out_specs=out_specs, check_vma=False
    )
```

```python
import math

import jax
import jax.numpy as jnp
from jax import lax
from jax.experimental import pallas as pl
from jax.experimental.pallas import tpu as pltpu
from jax.sharding import Mesh
from jax.sharding import PartitionSpec as P

D = 4096
HS = 128
ROT = 32
PT = 128
GROUP = 512
LH = 4
LW = LH * HS
SLOTS = 13
REQS = 8
MAXP = 36
TOK = 128
PIECES = LW + 32
COLS = D // 4
QW = 1536
NEG = -1e30
C2 = math.log2(math.e) / math.sqrt(HS)
F32 = jnp.float32
BF16 = jnp.bfloat16
VMEM = pltpu.VMEM
HBM = pltpu.HBM
SMEM = pltpu.SMEM


def whole(space=VMEM):
    return pl.BlockSpec(memory_space=space)


def limit(mib):
    return pltpu.CompilerParams(vmem_limit_bytes=mib << 20)


def head_rows(h):
    return slice(h * HS, (h + 1) * HS)


def rotary_kernel(info, lens, x_ref, rate_ref, q_ref, kv_ref):
    half = ROT // 2
    page = info[0]
    first = lens[lax.div(page, 4)] + lax.rem(page, 4) * TOK
    lane = lax.broadcasted_iota(jnp.int32, (half, TOK), 1)
    angles = (first + lane).astype(F32) * rate_ref[...]
    cosine = jnp.cos(angles)
    sine = jnp.sin(angles)
    for h in range(LH):
        for which in range(2):
            base = (3 * h + which) * HS
            turned = x_ref[:, base : base + HS].astype(F32).T
            a = turned[0:half]
            b = turned[half:ROT]
            done = jnp.concatenate(
                [a * cosine - b * sine, b * cosine + a * sine, turned[ROT:]], axis=0
            )
            if which == 0:
                q_ref[head_rows(h), :] = done.astype(BF16)
            else:
                kv_ref[:, head_rows(h)] = done.T.astype(BF16)
        base = (3 * h + 2) * HS
        kv_ref[:, LW + h * HS : LW + (h + 1) * HS] = x_ref[:, base : base + HS]


def rotary(info, lens, group_qkv, rates):
    return pl.pallas_call(
        rotary_kernel,
        out_shape=(
            jax.ShapeDtypeStruct((LW, TOK), BF16),
            jax.ShapeDtypeStruct((TOK, 2 * LW), BF16),
        ),
        in_specs=[whole(SMEM)] * 2 + [whole()] * 2,
        out_specs=(whole(), whole()),
        compiler_params=limit(2),
        name="rotary",
    )(info, lens, group_qkv, rates)


def stack_kernel(*refs):
    for i, ref in enumerate(refs[:-1]):
        refs[-1][i] = ref[...]


def stack(parts):
    return pl.pallas_call(
        stack_kernel,
        out_shape=jax.ShapeDtypeStruct((len(parts),) + parts[0].shape, parts[0].dtype),
        in_specs=[whole()] * len(parts),
        out_specs=whole(),
        compiler_params=limit(12),
        name="stack",
    )(*parts)


LIST = 32


def list_kernel(info, lens, table, codes, counts):
    core = info[3]
    first_slot = 2 * SLOTS * lax.div(info[0], 2)
    own_first = SLOTS * core

    def scan_request(request, carry):
        length = lens[request]
        found = jnp.int32(0)
        for g in range(LIST):
            slot = table[request, g] - first_slot
            here = (slot >= 0) & (slot < 2 * SLOTS) & (g * PT < length)
            local = slot - own_first
            codes[request, found] = g * LIST + jnp.where(local < 0, local + 2 * SLOTS, local)
            found = found + here.astype(jnp.int32)
        counts[request] = found
        return carry

    lax.fori_loop(0, REQS, scan_request, 0)


def page_lists(info, lens, table):
    return pl.pallas_call(
        list_kernel,
        out_shape=(
            jax.ShapeDtypeStruct((REQS, LIST + 1), jnp.int32),
            jax.ShapeDtypeStruct((REQS,), jnp.int32),
        ),
        in_specs=[whole(SMEM)] * 3,
        out_specs=(whole(SMEM), whole(SMEM)),
        compiler_params=limit(1),
        name="page_lists",
    )(info, lens, table)


def pool_kernel(k_other, v_other, keys, values, sems):
    copies = [
        pltpu.make_async_copy(src.at[i], dst.at[i], sems.at[n, i])
        for n, (src, dst) in enumerate(((k_other, keys), (v_other, values)))
        for i in range(SLOTS)
    ]
    for copy in copies:
        copy.start()
    for copy in copies:
        copy.wait()


def pool(k_other, v_other):
    shape = jax.ShapeDtypeStruct(k_other.shape, BF16)
    return pl.pallas_call(
        pool_kernel,
        out_shape=(shape, shape),
        in_specs=[whole(HBM)] * 2,
        out_specs=(whole(), whole()),
        scratch_shapes=[pltpu.SemaphoreType.DMA((2, SLOTS))],
        compiler_params=limit(8),
        name="pool",
    )(k_other, v_other)


PARTS = 32


def load_kernel(src, dst, sems):
    rows = src.shape[0] // PARTS
    copies = [
        pltpu.make_async_copy(
            src.at[pl.ds(i * rows, rows)], dst.at[pl.ds(i * rows, rows)], sems.at[i]
        )
        for i in range(PARTS)
    ]
    for copy in copies:
        copy.start()
    for copy in copies:
        copy.wait()


def load(array):
    return pl.pallas_call(
        load_kernel,
        out_shape=jax.ShapeDtypeStruct(array.shape, array.dtype),
        in_specs=[whole(HBM)],
        out_specs=whole(),
        scratch_shapes=[pltpu.SemaphoreType.DMA((PARTS,))],
        compiler_params=limit(40),
        name="load",
    )(array)


def split3(value):
    top = value.astype(BF16)
    rest = value - top.astype(F32)
    middle = rest.astype(BF16)
    low = (rest - middle.astype(F32)).astype(BF16)
    return top, middle, low


def stat_rows(stats):
    width = stats.shape[1]
    return jnp.concatenate(
        [piece.astype(F32) for piece in split3(stats)] + [jnp.zeros((8, width), F32)], axis=0
    ).astype(BF16)


def attention_kernel(
    step, info, lens, codes, counts, q_ref, k_own, v_own, k_other, v_other, *rest
):
    if step != 2:
        fresh_own, fresh_other, *rest = rest
    o_ref, acc, stats = rest
    y = info[1]
    x = info[2]
    core = info[3]
    key_row = lax.broadcasted_iota(jnp.int32, (2 * PT, TOK), 0)
    lane = lax.broadcasted_iota(jnp.int32, (2 * PT, TOK), 1)

    def block_loop(block, carry):
        row = lax.bitwise_and(y - jnp.where(core == 0, step, block), 3)
        column = lax.bitwise_and(x - jnp.where(core == 0, block, step), 3)
        request = 2 * row + lax.div(column, 2)

        def absorb(key_of, value_of, mask, guard):
            old = stats[...]
            scores = [
                jnp.where(
                    mask,
                    jnp.dot(key_of(h), q_ref[block, head_rows(h), :], preferred_element_type=F32),
                    NEG,
                )
                for h in range(LH)
            ]
            peaks = [
                jnp.maximum(old[h : h + 1], jnp.max(scores[h], axis=0, keepdims=True))
                for h in range(LH)
            ]
            weights = [jnp.exp2((scores[h] - peaks[h]) * C2) for h in range(LH)]
            if guard:
                weights = [jnp.where(mask, w, 0.0) for w in weights]
            decays = [jnp.exp2((old[h : h + 1] - peaks[h]) * C2) for h in range(LH)]
            totals = [
                old[LH + h : LH + h + 1] * decays[h] + jnp.sum(weights[h], axis=0, keepdims=True)
                for h in range(LH)
            ]
            stats[...] = jnp.concatenate(peaks + totals, axis=0)
            added = [
                lax.dot_general(
                    value_of(h), weights[h].astype(BF16), (((0,), (0,)), ((), ())),
                    preferred_element_type=F32,
                )
                for h in range(LH)
            ]
            for h in range(LH):
                acc[head_rows(h), :] = acc[head_rows(h), :] * decays[h] + added[h]

        acc[...] = jnp.zeros_like(acc)
        stats[...] = jnp.where(lax.broadcasted_iota(jnp.int32, (2 * LH, TOK), 0) < LH, NEG, 0.0)
        count = counts[request]

        def pages_step(i, inner):
            full = 2 * i + 1 < count
            first = codes[request, 2 * i]
            second = codes[request, jnp.where(full, 2 * i + 1, 2 * i)]
            lower = lens[request] - lax.div(first, LIST) * PT
            upper = jnp.where(full, lens[request] - lax.div(second, LIST) * PT, 0) + PT
            mask = key_row < jnp.where(key_row < PT, lower, upper)

            def page_rows(own, other, code, h):
                slot = lax.rem(code, LIST)
                mine = slot < SLOTS
                local = jnp.where(mine, slot, slot - SLOTS)
                return jnp.where(
                    mine, own[local, :, head_rows(h)], other[local, :, head_rows(h)]
                )

            def pair(own, other, h):
                return jnp.concatenate(
                    [page_rows(own, other, first, h), page_rows(own, other, second, h)], axis=0
                )

            absorb(
                lambda h: pair(k_own, k_other, h), lambda h: pair(v_own, v_other, h), mask, False
            )
            return inner

        lax.fori_loop(0, lax.div(count + 1, 2), pages_step, 0)
        if step != 2:

            @pl.when(request == 2 * y + lax.div(x, 2))
            def _():
                pair = lambda cols: jnp.concatenate(
                    [fresh_own[:, cols], fresh_other[:, cols]], axis=0
                )
                token = 2 * lax.bitwise_and(x, 1) * TOK + jnp.where(
                    key_row < PT, key_row + core * TOK, key_row - core * TOK
                )
                query = (2 * lax.bitwise_and(column, 1) + core) * TOK + lane
                absorb(
                    lambda h: pair(head_rows(h)),
                    lambda h: pair(slice(LW + h * HS, LW + (h + 1) * HS)),
                    token <= query,
                    True,
                )

        for h in range(LH):
            o_ref[block, head_rows(h), :] = acc[head_rows(h), :].astype(BF16)
        o_ref[block, LW:PIECES, :] = stat_rows(stats[...])
        return carry

    lax.fori_loop(0, 4, block_loop, 0)


def attend(step, info, lens, lists, queries, caches, fresh):
    operands = [info, lens, *lists, queries, *caches] + ([] if step == 2 else list(fresh))
    specs = [whole(SMEM)] * 4 + [whole()] * (5 if step == 2 else 7)

    def body(*refs):
        attention_kernel(step, *refs)

    return pl.pallas_call(
        body,
        out_shape=jax.ShapeDtypeStruct((4, PIECES, TOK), BF16),
        in_specs=specs,
        out_specs=whole(),
        scratch_shapes=[VMEM((LW, TOK), F32), VMEM((2 * LH, TOK), F32)],
        compiler_params=limit(12),
        cost_estimate=pl.CostEstimate(flops=0, transcendentals=0, bytes_accessed=0),
        name="attend%d" % step,
    )(*operands)


def join(parts):
    read = []
    for part in parts:
        tail = part[LW:PIECES].astype(F32)
        read.append(tail[0:8] + tail[8:16] + tail[16:24])
    peak = read[0][0:LH]
    for value in read[1:]:
        peak = jnp.maximum(peak, value[0:LH])
    factors = [jnp.exp2((value[0:LH] - peak) * C2) for value in read]
    total = sum(value[LH : 2 * LH] * factor for value, factor in zip(read, factors))
    weighted = [
        sum(
            part[head_rows(h)].astype(F32) * factor[h : h + 1]
            for part, factor in zip(parts, factors)
        )
        for h in range(LH)
    ]
    return peak, total, weighted


def join_rows_kernel(a_ref, b_ref, c_ref, d_ref, *outs):
    for block, out in enumerate(outs):
        parts = [ref.at[block] for ref in (a_ref, b_ref, c_ref, d_ref)]
        peak, total, weighted = join(parts)
        for h in range(LH):
            out[head_rows(h), :] = weighted[h].astype(BF16)
        out[LW:PIECES, :] = stat_rows(jnp.concatenate([peak, total], axis=0))


def join_last_kernel(a_ref, b_ref, c_ref, d_ref, out):
    _, total, weighted = join([a_ref, b_ref, c_ref, d_ref])
    inverse = 1.0 / total
    for h in range(LH):
        out[:, head_rows(h)] = (weighted[h] * inverse[h : h + 1]).T.astype(BF16)


def join_rows(parts):
    return pl.pallas_call(
        join_rows_kernel,
        out_shape=tuple(jax.ShapeDtypeStruct((PIECES, TOK), BF16) for _ in range(4)),
        in_specs=[whole()] * 4,
        out_specs=tuple(whole() for _ in range(4)),
        compiler_params=limit(8),
        name="join_rows",
    )(*parts)


def join_last(parts):
    return pl.pallas_call(
        join_last_kernel,
        out_shape=jax.ShapeDtypeStruct((TOK, LW), BF16),
        in_specs=[whole()] * 4,
        out_specs=whole(),
        compiler_params=limit(4),
        name="join_last",
    )(*parts)


def dense_kernel(info, attention, weight, bias, hidden, branch, own, *outs):
    head = info[4]
    base = pl.ds(pl.multiple_of(head * COLS, COLS), COLS)
    for s in range(4):
        target = lax.bitwise_and(head + s, 3)
        cols = pl.ds(pl.multiple_of(target * COLS, COLS), COLS)
        product = jnp.dot(attention[...], weight[:, cols], preferred_element_type=F32)
        if s == 0:
            rest = bias[base].reshape(1, COLS) + hidden[...].astype(F32) + branch[...].astype(F32)
            own[...] = product + rest
        else:
            outs[s - 1][...] = product.astype(BF16)


def dense(info, attention, weight, bias, hidden, branch):
    shape = jax.ShapeDtypeStruct((TOK, COLS), BF16)
    return pl.pallas_call(
        dense_kernel,
        out_shape=(jax.ShapeDtypeStruct((TOK, COLS), F32), shape, shape, shape),
        in_specs=[whole(SMEM)] + [whole()] * 5,
        out_specs=(whole(),) * 4,
        compiler_params=limit(10),
        name="dense",
    )(info, attention, weight, bias, hidden, branch)


def join_shares_kernel(own, a, b, c, out):
    out[...] = (
        own[...] + (a[...].astype(F32) + b[...].astype(F32) + c[...].astype(F32))
    ).astype(BF16)


def join_shares(parts):
    return pl.pallas_call(
        join_shares_kernel,
        out_shape=jax.ShapeDtypeStruct((TOK, COLS), BF16),
        in_specs=[whole()] * 4,
        out_specs=whole(),
        compiler_params=limit(4),
        name="join_shares",
    )(*parts)


def qkv_kernel(info, x0, x1, x2, x3, gain, shift, weight, bias, out):
    head = info[4]
    blocks = (x0, x1, x2, x3)
    total = 0.0
    square = 0.0
    for block in blocks:
        value = block[...].astype(F32)
        total = total + jnp.sum(value, axis=1, keepdims=True)
        square = square + jnp.sum(value * value, axis=1, keepdims=True)
    mean = total / D
    variance = square / D - mean * mean
    scale = lax.rsqrt(variance + 1e-05)
    result = bias[...].reshape(1, QW) + jnp.zeros((TOK, QW), F32)
    for s, block in enumerate(blocks):
        origin = lax.bitwise_and(head - s, 3)
        rows = pl.ds(pl.multiple_of(origin * COLS, COLS), COLS)
        normed = (block[...].astype(F32) - mean) * scale * gain[rows].reshape(1, COLS)
        normed = (normed + shift[rows].reshape(1, COLS)).astype(BF16)
        result = result + jnp.dot(normed, weight[rows, :], preferred_element_type=F32)
    out[...] = result.astype(BF16)


def project_qkv(info, blocks, gain, shift, weight, bias):
    return pl.pallas_call(
        qkv_kernel,
        out_shape=jax.ShapeDtypeStruct((TOK, QW), BF16),
        in_specs=[whole(SMEM)] + [whole()] * 8,
        out_specs=whole(),
        compiler_params=limit(20),
        name="project_qkv",
    )(info, *blocks, gain, shift, weight, bias)


WINDOW = 2 * TOK


def patch_kernel(info, lens, table, *refs):
    news = refs[0:2]
    k_in, v_in, k_out, v_out, src, kbuf, vbuf, sems, bulk, slots, offsets = refs[2:]
    page = info[0]
    y = info[1]
    x = info[2]
    core = info[3]
    whole_copies = (
        pltpu.make_async_copy(k_in, k_out, bulk.at[0]),
        pltpu.make_async_copy(v_in, v_out, bulk.at[1]),
    )
    for copy in whole_copies:
        copy.start()

    def source(n, half, ref, outer, inner):
        return pltpu.make_async_copy(
            ref.at[outer, inner], src.at[n, pl.ds(half * TOK, TOK), :], sems.at[n, half]
        )

    def loads(n, local):
        return (
            pltpu.make_async_copy(k_in.at[local], kbuf.at[n], sems.at[n, 2]),
            pltpu.make_async_copy(v_in.at[local], vbuf.at[n], sems.at[n, 3]),
        )

    def stores(n, local):
        return (
            pltpu.make_async_copy(kbuf.at[n], k_out.at[local], sems.at[n, 4]),
            pltpu.make_async_copy(vbuf.at[n], v_out.at[local], sems.at[n, 5]),
        )

    def scan_request(request, count):
        length = lens[request]
        first = lax.div(length, PT)
        last = lax.div(length + (GROUP - 1), PT)

        def scan(g, n):
            slot = table[request, g]
            here = lax.div(slot, SLOTS) == page

            @pl.when(here)
            def _():
                local = slot - page * SLOTS
                offset = g * PT - length
                lower = lax.div(offset + PT, PT) - 1
                slots[n] = local
                offsets[n] = offset
                for copy in loads(n, local):
                    copy.start()
                row_shift = lax.bitwise_and(y - lax.div(request, 2), 3)
                for half in range(2):
                    block = jnp.clip(lower + half, 0, 3)
                    column = 2 * lax.rem(request, 2) + lax.div(block, 2)
                    column_shift = lax.bitwise_and(x - column, 3)
                    origin = lax.rem(block, 2)
                    inner = jnp.where(origin == 0, column_shift, row_shift)
                    outer = jnp.where(origin == 0, row_shift, column_shift)

                    @pl.when(origin == core)
                    def _(half=half, outer=outer, inner=inner):
                        source(n, half, news[0], outer, inner).start()

                    @pl.when(origin != core)
                    def _(half=half, outer=outer, inner=inner):
                        source(n, half, news[1], outer, inner).start()

            return n + here.astype(jnp.int32)

        return lax.fori_loop(first, last + 1, scan, count)

    count = lax.fori_loop(0, REQS, scan_request, jnp.int32(0))
    pick_row = lax.broadcasted_iota(jnp.int32, (PT, WINDOW), 0)
    pick_col = lax.broadcasted_iota(jnp.int32, (PT, WINDOW), 1)
    token = lax.broadcasted_iota(jnp.int32, (PT, LW), 0)

    def update(n, carry):
        for half in range(2):
            source(n, half, news[0], 0, 0).wait()
        for copy in loads(n, 0):
            copy.wait()
        offset = offsets[n]
        base = (lax.div(offset + PT, PT) - 1) * PT
        pick = jnp.where(pick_col == pick_row + (offset - base), 1.0, 0.0).astype(BF16)
        index = token + offset
        fresh = (index >= 0) & (index < GROUP)
        for buf, cols in ((kbuf, slice(0, LW)), (vbuf, slice(LW, 2 * LW))):
            moved = jnp.dot(pick, src[n, :, cols], preferred_element_type=F32)
            buf[n] = jnp.where(fresh, moved, buf[n].astype(F32)).astype(BF16)
        return carry

    def put(n, carry):
        for copy in stores(n, slots[n]):
            copy.start()
        return carry

    def finish(n, carry):
        for copy in stores(n, 0):
            copy.wait()
        return carry

    lax.fori_loop(0, count, update, 0)
    for copy in whole_copies:
        copy.wait()
    lax.fori_loop(0, count, put, 0)
    lax.fori_loop(0, count, finish, 0)


def patch(info, lens, table, news, key_cache, value_cache):
    shape = jax.ShapeDtypeStruct(key_cache.shape, BF16)
    return pl.pallas_call(
        patch_kernel,
        out_shape=(shape, shape),
        in_specs=[whole(SMEM)] * 3 + [whole(HBM)] * 4,
        out_specs=(whole(HBM), whole(HBM)),
        scratch_shapes=[
            VMEM((SLOTS, WINDOW, 2 * LW), BF16),
            VMEM((SLOTS, PT, LW), BF16),
            VMEM((SLOTS, PT, LW), BF16),
            pltpu.SemaphoreType.DMA((SLOTS, 6)),
            pltpu.SemaphoreType.DMA((2,)),
            SMEM((SLOTS,), jnp.int32),
            SMEM((SLOTS,), jnp.int32),
        ],
        compiler_params=pltpu.CompilerParams(vmem_limit_bytes=20 << 20),
        name="patch",
    )(info, lens, table, *news, key_cache, value_cache)


def shift(s):
    return [(i, (i + s) % 4) for i in range(4)]


PLANE = ("y", "x", "core")
CORES = [(0, 1), (1, 0)]


def plane_shift(s, stage):
    pairs = []
    for y in range(4):
        for x in range(4):
            for c in range(2):
                along_x = (c == 0) == (stage == 0)
                to_y, to_x = (y, (x + s) % 4) if along_x else ((y + s) % 4, x)
                pairs.append((y * 8 + x * 2 + c, to_y * 8 + to_x * 2 + c))
    return pairs


def send(array, s, stage):
    return lax.ppermute(array, PLANE, plane_shift(s, stage))


def on_device(
    hidden,
    group_qkv,
    mlp_branch,
    key_cache,
    paged_value_cache,
    cache_lengths,
    page_table,
    dense_weight,
    dense_bias,
    norm_gain,
    norm_bias,
    qkv_weight,
    qkv_bias,
):
    y = lax.axis_index("y").astype(jnp.int32)
    x = lax.axis_index("x").astype(jnp.int32)
    core = lax.axis_index("core").astype(jnp.int32)
    head = lax.axis_index("head").astype(jnp.int32)
    page = 8 * y + 2 * x + core

    info = jnp.stack([page, y, x, core, head])

    inverse = 1.0 / 10000.0 ** (jnp.arange(0, ROT, 2, dtype=F32) / ROT)
    rates = jnp.broadcast_to(inverse[:, None], (ROT // 2, TOK))
    queries, fresh = rotary(info, cache_lengths, group_qkv, rates)

    other_keys = lax.ppermute(key_cache, "core", CORES)
    other_values = lax.ppermute(paged_value_cache, "core", CORES)
    other_fresh = lax.ppermute(fresh, "core", CORES)
    near = [queries] + [send(queries, s, 0) for s in range(1, 4)]
    codes, counts = page_lists(info, cache_lengths, page_table)
    pool_keys, pool_values = pool(other_keys, other_values)
    near, codes, pool_keys = lax.optimization_barrier((near, codes, pool_keys))
    near = stack(near)
    all_queries = [near] + [send(near, s, 1) for s in range(1, 4)]

    late_fresh, _ = lax.optimization_barrier((fresh, near))
    new_rows = [fresh] + [send(late_fresh, s, 0) for s in range(1, 4)]
    caches = (key_cache, paged_value_cache, pool_keys, pool_values)

    partials = [None] * 4
    last = None
    for s in (0, 1, 3, 2):
        wanted = all_queries[s]
        if last is not None:
            wanted, last = lax.optimization_barrier((wanted, last))
        part = attend(
            s, info, cache_lengths, (codes, counts), wanted, caches, (fresh, other_fresh)
        )
        if last is not None:
            partials[before] = last if before == 0 else send(last, -before, 1)
        last, before = part, s
    partials[before] = send(last, -before, 1)
    blocks = join_rows(partials)
    new_rows = stack(new_rows)
    blocks, new_rows = lax.optimization_barrier((blocks, new_rows))
    from_left = send(new_rows, 1, 1)
    from_right = send(new_rows, 3, 1)
    blocks = [blocks[0]] + [send(blocks[s], -s, 0) for s in range(1, 4)]
    attention = join_last(blocks)

    shares = dense(info, attention, dense_weight, dense_bias, hidden, mlp_branch)
    shares = [shares[0]] + [lax.ppermute(shares[s], "head", shift(s)) for s in range(1, 4)]
    (from_left, from_right, new_rows), _ = lax.optimization_barrier(
        ((from_left, from_right, new_rows), shares[0])
    )
    opposite = send(from_left, 1, 1)
    new_hidden = join_shares(shares)
    (opposite, new_rows), _ = lax.optimization_barrier(((opposite, new_rows), new_hidden))
    gathered = stack([new_rows, from_left, opposite, from_right])
    news = (gathered, lax.ppermute(gathered, "core", CORES))

    streams = [new_hidden] + [lax.ppermute(new_hidden, "head", shift(s)) for s in range(1, 4)]
    late_weight, _ = lax.optimization_barrier((qkv_weight, new_hidden))
    next_qkv = project_qkv(
        info, streams, norm_gain, norm_bias, load(late_weight), qkv_bias
    )

    key_out, value_out = patch(
        info, cache_lengths, page_table, news, key_cache, paged_value_cache
    )
    return (new_hidden, next_qkv, key_out, value_out)


def solution(mesh):
    plane = PLANE
    fine = Mesh(mesh.devices.reshape(4, 4, 4, 2), ("head",) + plane)
    in_specs = (
        P(plane, "head"),
        P(plane, "head"),
        P(plane, "head"),
        P(plane, None, "head"),
        P(plane, None, "head"),
        P(),
        P(),
        P("head", None),
        P(),
        P(),
        P(),
        P(None, "head"),
        P("head"),
    )
    out_specs = (
        P(plane, "head"),
        P(plane, "head"),
        P(plane, None, "head"),
        P(plane, None, "head"),
    )
    return jax.shard_map(
        on_device, mesh=fine, in_specs=in_specs, out_specs=out_specs, check_vma=False
    )
```

```python
import math

import jax
import jax.numpy as jnp
from jax import lax
from jax.experimental import pallas as pl
from jax.experimental.pallas import tpu as pltpu
from jax.sharding import Mesh
from jax.sharding import PartitionSpec as P

D = 4096
HS = 128
ROT = 32
PT = 128
GROUP = 512
LH = 4
LW = LH * HS
SLOTS = 13
REQS = 8
MAXP = 36
TOK = 128
PIECES = LW + 32
COLS = D // 4
QW = 1536
NEG = -1e30
C2 = math.log2(math.e) / math.sqrt(HS)
F32 = jnp.float32
BF16 = jnp.bfloat16
VMEM = pltpu.VMEM
HBM = pltpu.HBM
SMEM = pltpu.SMEM


def whole(space=VMEM):
    return pl.BlockSpec(memory_space=space)


def limit(mib):
    return pltpu.CompilerParams(vmem_limit_bytes=mib << 20)


def head_rows(h):
    return slice(h * HS, (h + 1) * HS)


def rotary_kernel(info, lens, x_ref, rate_ref, q_ref, kv_ref):
    half = ROT // 2
    page = info[0]
    first = lens[lax.div(page, 4)] + lax.rem(page, 4) * TOK
    lane = lax.broadcasted_iota(jnp.int32, (half, TOK), 1)
    angles = (first + lane).astype(F32) * rate_ref[...]
    cosine = jnp.cos(angles)
    sine = jnp.sin(angles)
    for h in range(LH):
        for which in range(2):
            base = (3 * h + which) * HS
            turned = x_ref[:, base : base + HS].astype(F32).T
            a = turned[0:half]
            b = turned[half:ROT]
            done = jnp.concatenate(
                [a * cosine - b * sine, b * cosine + a * sine, turned[ROT:]], axis=0
            )
            if which == 0:
                q_ref[head_rows(h), :] = done.astype(BF16)
            else:
                kv_ref[:, head_rows(h)] = done.T.astype(BF16)
        base = (3 * h + 2) * HS
        kv_ref[:, LW + h * HS : LW + (h + 1) * HS] = x_ref[:, base : base + HS]


def rotary(info, lens, group_qkv, rates):
    return pl.pallas_call(
        rotary_kernel,
        out_shape=(
            jax.ShapeDtypeStruct((LW, TOK), BF16),
            jax.ShapeDtypeStruct((TOK, 2 * LW), BF16),
        ),
        in_specs=[whole(SMEM)] * 2 + [whole()] * 2,
        out_specs=(whole(), whole()),
        compiler_params=limit(2),
        name="rotary",
    )(info, lens, group_qkv, rates)


def stack_kernel(*refs):
    for i, ref in enumerate(refs[:-1]):
        refs[-1][i] = ref[...]


def stack(parts):
    return pl.pallas_call(
        stack_kernel,
        out_shape=jax.ShapeDtypeStruct((len(parts),) + parts[0].shape, parts[0].dtype),
        in_specs=[whole()] * len(parts),
        out_specs=whole(),
        compiler_params=limit(12),
        name="stack",
    )(*parts)


LIST = 32


def list_kernel(info, lens, table, codes, counts):
    core = info[3]
    first_slot = 2 * SLOTS * lax.div(info[0], 2)
    own_first = SLOTS * core

    def scan_request(request, carry):
        length = lens[request]
        found = jnp.int32(0)
        for g in range(LIST):
            slot = table[request, g] - first_slot
            here = (slot >= 0) & (slot < 2 * SLOTS) & (g * PT < length)
            local = slot - own_first
            codes[request, found] = g * LIST + jnp.where(local < 0, local + 2 * SLOTS, local)
            found = found + here.astype(jnp.int32)
        counts[request] = found
        return carry

    lax.fori_loop(0, REQS, scan_request, 0)


def page_lists(info, lens, table):
    return pl.pallas_call(
        list_kernel,
        out_shape=(
            jax.ShapeDtypeStruct((REQS, LIST + 1), jnp.int32),
            jax.ShapeDtypeStruct((REQS,), jnp.int32),
        ),
        in_specs=[whole(SMEM)] * 3,
        out_specs=(whole(SMEM), whole(SMEM)),
        compiler_params=limit(1),
        name="page_lists",
    )(info, lens, table)


def pool_kernel(k_other, v_other, keys, values, sems):
    copies = [
        pltpu.make_async_copy(src.at[i], dst.at[i], sems.at[n, i])
        for n, (src, dst) in enumerate(((k_other, keys), (v_other, values)))
        for i in range(SLOTS)
    ]
    for copy in copies:
        copy.start()
    for copy in copies:
        copy.wait()


def pool(k_other, v_other):
    shape = jax.ShapeDtypeStruct(k_other.shape, BF16)
    return pl.pallas_call(
        pool_kernel,
        out_shape=(shape, shape),
        in_specs=[whole(HBM)] * 2,
        out_specs=(whole(), whole()),
        scratch_shapes=[pltpu.SemaphoreType.DMA((2, SLOTS))],
        compiler_params=limit(8),
        name="pool",
    )(k_other, v_other)


PARTS = 32


def load_kernel(src, dst, sems):
    rows = src.shape[0] // PARTS
    copies = [
        pltpu.make_async_copy(
            src.at[pl.ds(i * rows, rows)], dst.at[pl.ds(i * rows, rows)], sems.at[i]
        )
        for i in range(PARTS)
    ]
    for copy in copies:
        copy.start()
    for copy in copies:
        copy.wait()


def load(array):
    return pl.pallas_call(
        load_kernel,
        out_shape=jax.ShapeDtypeStruct(array.shape, array.dtype),
        in_specs=[whole(HBM)],
        out_specs=whole(),
        scratch_shapes=[pltpu.SemaphoreType.DMA((PARTS,))],
        compiler_params=limit(40),
        name="load",
    )(array)


def split3(value):
    top = value.astype(BF16)
    rest = value - top.astype(F32)
    middle = rest.astype(BF16)
    low = (rest - middle.astype(F32)).astype(BF16)
    return top, middle, low


def stat_rows(stats):
    width = stats.shape[1]
    return jnp.concatenate(
        [piece.astype(F32) for piece in split3(stats)] + [jnp.zeros((8, width), F32)], axis=0
    ).astype(BF16)


def attention_kernel(
    step, info, lens, codes, counts, q_ref, k_own, v_own, k_other, v_other, *rest
):
    if step != 2:
        fresh_own, fresh_other, *rest = rest
    o_ref, acc, stats = rest
    y = info[1]
    x = info[2]
    core = info[3]
    key_row = lax.broadcasted_iota(jnp.int32, (2 * PT, TOK), 0)
    lane = lax.broadcasted_iota(jnp.int32, (2 * PT, TOK), 1)

    def block_loop(block, carry):
        row = lax.bitwise_and(y - jnp.where(core == 0, step, block), 3)
        column = lax.bitwise_and(x - jnp.where(core == 0, block, step), 3)
        request = 2 * row + lax.div(column, 2)

        def absorb(key_of, value_of, mask, guard):
            old = stats[...]
            scores = [
                jnp.where(
                    mask,
                    jnp.dot(key_of(h), q_ref[block, head_rows(h), :], preferred_element_type=F32),
                    NEG,
                )
                for h in range(LH)
            ]
            peaks = [
                jnp.maximum(old[h : h + 1], jnp.max(scores[h], axis=0, keepdims=True))
                for h in range(LH)
            ]
            weights = [jnp.exp2((scores[h] - peaks[h]) * C2) for h in range(LH)]
            if guard:
                weights = [jnp.where(mask, w, 0.0) for w in weights]
            decays = [jnp.exp2((old[h : h + 1] - peaks[h]) * C2) for h in range(LH)]
            totals = [
                old[LH + h : LH + h + 1] * decays[h] + jnp.sum(weights[h], axis=0, keepdims=True)
                for h in range(LH)
            ]
            stats[...] = jnp.concatenate(peaks + totals, axis=0)
            added = [
                lax.dot_general(
                    value_of(h), weights[h].astype(BF16), (((0,), (0,)), ((), ())),
                    preferred_element_type=F32,
                )
                for h in range(LH)
            ]
            for h in range(LH):
                acc[head_rows(h), :] = acc[head_rows(h), :] * decays[h] + added[h]

        acc[...] = jnp.zeros_like(acc)
        stats[...] = jnp.where(lax.broadcasted_iota(jnp.int32, (2 * LH, TOK), 0) < LH, NEG, 0.0)
        count = counts[request]

        def pages_step(i, inner):
            full = 2 * i + 1 < count
            first = codes[request, 2 * i]
            second = codes[request, jnp.where(full, 2 * i + 1, 2 * i)]
            lower = lens[request] - lax.div(first, LIST) * PT
            upper = jnp.where(full, lens[request] - lax.div(second, LIST) * PT, 0) + PT
            mask = key_row < jnp.where(key_row < PT, lower, upper)

            def page_rows(own, other, code, h):
                slot = lax.rem(code, LIST)
                mine = slot < SLOTS
                local = jnp.where(mine, slot, slot - SLOTS)
                return jnp.where(
                    mine, own[local, :, head_rows(h)], other[local, :, head_rows(h)]
                )

            def pair(own, other, h):
                return jnp.concatenate(
                    [page_rows(own, other, first, h), page_rows(own, other, second, h)], axis=0
                )

            absorb(
                lambda h: pair(k_own, k_other, h), lambda h: pair(v_own, v_other, h), mask, False
            )
            return inner

        lax.fori_loop(0, lax.div(count + 1, 2), pages_step, 0)
        if step != 2:

            @pl.when(request == 2 * y + lax.div(x, 2))
            def _():
                pair = lambda cols: jnp.concatenate(
                    [fresh_own[:, cols], fresh_other[:, cols]], axis=0
                )
                token = 2 * lax.bitwise_and(x, 1) * TOK + jnp.where(
                    key_row < PT, key_row + core * TOK, key_row - core * TOK
                )
                query = (2 * lax.bitwise_and(column, 1) + core) * TOK + lane
                absorb(
                    lambda h: pair(head_rows(h)),
                    lambda h: pair(slice(LW + h * HS, LW + (h + 1) * HS)),
                    token <= query,
                    True,
                )

        for h in range(LH):
            o_ref[block, head_rows(h), :] = acc[head_rows(h), :].astype(BF16)
        o_ref[block, LW:PIECES, :] = stat_rows(stats[...])
        return carry

    lax.fori_loop(0, 4, block_loop, 0)


def attend(step, info, lens, lists, queries, caches, fresh):
    operands = [info, lens, *lists, queries, *caches] + ([] if step == 2 else list(fresh))
    specs = [whole(SMEM)] * 4 + [whole()] * (5 if step == 2 else 7)

    def body(*refs):
        attention_kernel(step, *refs)

    return pl.pallas_call(
        body,
        out_shape=jax.ShapeDtypeStruct((4, PIECES, TOK), BF16),
        in_specs=specs,
        out_specs=whole(),
        scratch_shapes=[VMEM((LW, TOK), F32), VMEM((2 * LH, TOK), F32)],
        compiler_params=limit(12),
        cost_estimate=pl.CostEstimate(flops=0, transcendentals=0, bytes_accessed=0),
        name="attend%d" % step,
    )(*operands)


def join(parts):
    read = []
    for part in parts:
        tail = part[LW:PIECES].astype(F32)
        read.append(tail[0:8] + tail[8:16] + tail[16:24])
    peak = read[0][0:LH]
    for value in read[1:]:
        peak = jnp.maximum(peak, value[0:LH])
    factors = [jnp.exp2((value[0:LH] - peak) * C2) for value in read]
    total = sum(value[LH : 2 * LH] * factor for value, factor in zip(read, factors))
    weighted = [
        sum(
            part[head_rows(h)].astype(F32) * factor[h : h + 1]
            for part, factor in zip(parts, factors)
        )
        for h in range(LH)
    ]
    return peak, total, weighted


def join_rows_kernel(a_ref, b_ref, c_ref, d_ref, *outs):
    for block, out in enumerate(outs):
        parts = [ref.at[block] for ref in (a_ref, b_ref, c_ref, d_ref)]
        peak, total, weighted = join(parts)
        for h in range(LH):
            out[head_rows(h), :] = weighted[h].astype(BF16)
        out[LW:PIECES, :] = stat_rows(jnp.concatenate([peak, total], axis=0))


def join_last_kernel(a_ref, b_ref, c_ref, d_ref, out):
    _, total, weighted = join([a_ref, b_ref, c_ref, d_ref])
    inverse = 1.0 / total
    for h in range(LH):
        out[:, head_rows(h)] = (weighted[h] * inverse[h : h + 1]).T.astype(BF16)


def join_rows(parts):
    return pl.pallas_call(
        join_rows_kernel,
        out_shape=tuple(jax.ShapeDtypeStruct((PIECES, TOK), BF16) for _ in range(4)),
        in_specs=[whole()] * 4,
        out_specs=tuple(whole() for _ in range(4)),
        compiler_params=limit(8),
        name="join_rows",
    )(*parts)


def join_last(parts):
    return pl.pallas_call(
        join_last_kernel,
        out_shape=jax.ShapeDtypeStruct((TOK, LW), BF16),
        in_specs=[whole()] * 4,
        out_specs=whole(),
        compiler_params=limit(4),
        name="join_last",
    )(*parts)


def dense_kernel(info, attention, weight, bias, hidden, branch, own, *outs):
    head = info[4]
    base = pl.ds(pl.multiple_of(head * COLS, COLS), COLS)
    for s in range(4):
        target = lax.bitwise_and(head + s, 3)
        cols = pl.ds(pl.multiple_of(target * COLS, COLS), COLS)
        product = jnp.dot(attention[...], weight[:, cols], preferred_element_type=F32)
        if s == 0:
            rest = bias[base].reshape(1, COLS) + hidden[...].astype(F32) + branch[...].astype(F32)
            own[...] = product + rest
        else:
            outs[s - 1][...] = product.astype(BF16)


def dense(info, attention, weight, bias, hidden, branch):
    shape = jax.ShapeDtypeStruct((TOK, COLS), BF16)
    return pl.pallas_call(
        dense_kernel,
        out_shape=(jax.ShapeDtypeStruct((TOK, COLS), F32), shape, shape, shape),
        in_specs=[whole(SMEM)] + [whole()] * 5,
        out_specs=(whole(),) * 4,
        compiler_params=limit(10),
        name="dense",
    )(info, attention, weight, bias, hidden, branch)


def join_shares_kernel(own, a, b, c, out):
    out[...] = (
        own[...] + (a[...].astype(F32) + b[...].astype(F32) + c[...].astype(F32))
    ).astype(BF16)


def join_shares(parts):
    return pl.pallas_call(
        join_shares_kernel,
        out_shape=jax.ShapeDtypeStruct((TOK, COLS), BF16),
        in_specs=[whole()] * 4,
        out_specs=whole(),
        compiler_params=limit(4),
        name="join_shares",
    )(*parts)


def qkv_kernel(info, token, x0, x1, x2, x3, gain, shift, weight, bias, out):
    head = info[4]
    blocks = (x0, x1, x2, x3)
    total = 0.0
    square = 0.0
    for block in blocks:
        value = block[...].astype(F32)
        total = total + jnp.sum(value, axis=1, keepdims=True)
        square = square + jnp.sum(value * value, axis=1, keepdims=True)
    mean = total / D
    variance = square / D - mean * mean
    scale = lax.rsqrt(variance + 1e-05)
    result = bias[...].reshape(1, QW) + jnp.zeros((TOK, QW), F32)
    for s, block in enumerate(blocks):
        origin = lax.bitwise_and(head - s, 3)
        rows = pl.ds(pl.multiple_of(origin * COLS, COLS), COLS)
        normed = (block[...].astype(F32) - mean) * scale * gain[rows].reshape(1, COLS)
        normed = (normed + shift[rows].reshape(1, COLS)).astype(BF16)
        result = result + jnp.dot(normed, weight[rows, :], preferred_element_type=F32)
    out[...] = result.astype(BF16)


def project_qkv(info, token, blocks, gain, shift, weight, bias):
    return pl.pallas_call(
        qkv_kernel,
        out_shape=jax.ShapeDtypeStruct((TOK, QW), BF16),
        in_specs=[whole(SMEM)] * 2 + [whole()] * 8,
        out_specs=whole(),
        compiler_params=limit(20),
        name="project_qkv",
    )(info, token, *blocks, gain, shift, weight, bias)


WINDOW = 2 * TOK


def patch_kernel(info, lens, table, *refs):
    news = refs[0:2]
    k_in, v_in, k_out, v_out, token_out, src, kbuf, vbuf, sems, bulk, slots, offsets = refs[2:]
    page = info[0]
    y = info[1]
    x = info[2]
    core = info[3]
    whole_copies = (
        pltpu.make_async_copy(k_in, k_out, bulk.at[0]),
        pltpu.make_async_copy(v_in, v_out, bulk.at[1]),
    )
    for copy in whole_copies:
        copy.start()

    def source(n, half, ref, outer, inner):
        return pltpu.make_async_copy(
            ref.at[outer, inner], src.at[n, pl.ds(half * TOK, TOK), :], sems.at[n, half]
        )

    def loads(n, local):
        return (
            pltpu.make_async_copy(k_in.at[local], kbuf.at[n], sems.at[n, 2]),
            pltpu.make_async_copy(v_in.at[local], vbuf.at[n], sems.at[n, 3]),
        )

    def stores(n, local):
        return (
            pltpu.make_async_copy(kbuf.at[n], k_out.at[local], sems.at[n, 4]),
            pltpu.make_async_copy(vbuf.at[n], v_out.at[local], sems.at[n, 5]),
        )

    def scan_request(request, count):
        length = lens[request]
        first = lax.div(length, PT)
        last = lax.div(length + (GROUP - 1), PT)

        def scan(g, n):
            slot = table[request, g]
            here = lax.div(slot, SLOTS) == page

            @pl.when(here)
            def _():
                local = slot - page * SLOTS
                offset = g * PT - length
                lower = lax.div(offset + PT, PT) - 1
                slots[n] = local
                offsets[n] = offset
                for copy in loads(n, local):
                    copy.start()
                row = lax.div(request, 2)
                for half in range(2):
                    block = jnp.clip(lower + half, 0, 3)
                    column = 2 * lax.rem(request, 2) + lax.div(block, 2)
                    origin = lax.rem(block, 2)
                    inner = jnp.where(origin == 0, column ^ x, row ^ y)
                    inner = inner ^ lax.div(inner, 2)
                    outer = lax.bitwise_and(jnp.where(origin == 0, y - row, x - column), 3)

                    @pl.when(origin == core)
                    def _(half=half, outer=outer, inner=inner):
                        source(n, half, news[0], outer, inner).start()

                    @pl.when(origin != core)
                    def _(half=half, outer=outer, inner=inner):
                        source(n, half, news[1], outer, inner).start()

            return n + here.astype(jnp.int32)

        return lax.fori_loop(first, last + 1, scan, count)

    count = lax.fori_loop(0, REQS, scan_request, jnp.int32(0))
    token_out[0] = count
    pick_row = lax.broadcasted_iota(jnp.int32, (PT, WINDOW), 0)
    pick_col = lax.broadcasted_iota(jnp.int32, (PT, WINDOW), 1)
    token = lax.broadcasted_iota(jnp.int32, (PT, LW), 0)

    def update(n, carry):
        for half in range(2):
            source(n, half, news[0], 0, 0).wait()
        for copy in loads(n, 0):
            copy.wait()
        offset = offsets[n]
        base = (lax.div(offset + PT, PT) - 1) * PT
        pick = jnp.where(pick_col == pick_row + (offset - base), 1.0, 0.0).astype(BF16)
        index = token + offset
        fresh = (index >= 0) & (index < GROUP)
        for buf, cols in ((kbuf, slice(0, LW)), (vbuf, slice(LW, 2 * LW))):
            moved = jnp.dot(pick, src[n, :, cols], preferred_element_type=F32)
            buf[n] = jnp.where(fresh, moved, buf[n].astype(F32)).astype(BF16)
        return carry

    def put(n, carry):
        for copy in stores(n, slots[n]):
            copy.start()
        return carry

    def finish(n, carry):
        for copy in stores(n, 0):
            copy.wait()
        return carry

    lax.fori_loop(0, count, update, 0)
    for copy in whole_copies:
        copy.wait()
    lax.fori_loop(0, count, put, 0)
    lax.fori_loop(0, count, finish, 0)


def patch(info, lens, table, news, key_cache, value_cache):
    shape = jax.ShapeDtypeStruct(key_cache.shape, BF16)
    return pl.pallas_call(
        patch_kernel,
        out_shape=(shape, shape, jax.ShapeDtypeStruct((1,), jnp.int32)),
        in_specs=[whole(SMEM)] * 3 + [whole(HBM)] * 4,
        out_specs=(whole(HBM), whole(HBM), whole(SMEM)),
        scratch_shapes=[
            VMEM((SLOTS, WINDOW, 2 * LW), BF16),
            VMEM((SLOTS, PT, LW), BF16),
            VMEM((SLOTS, PT, LW), BF16),
            pltpu.SemaphoreType.DMA((SLOTS, 6)),
            pltpu.SemaphoreType.DMA((2,)),
            SMEM((SLOTS,), jnp.int32),
            SMEM((SLOTS,), jnp.int32),
        ],
        compiler_params=pltpu.CompilerParams(vmem_limit_bytes=20 << 20),
        name="patch",
    )(info, lens, table, *news, key_cache, value_cache)


def shift(s):
    return [(i, (i + s) % 4) for i in range(4)]


PLANE = ("y", "x", "core")
CORES = [(0, 1), (1, 0)]


def plane_pairs(target, stage):
    pairs = []
    for y in range(4):
        for x in range(4):
            for c in range(2):
                along_x = (c == 0) == (stage == 0)
                to_y, to_x = (y, target(x)) if along_x else (target(y), x)
                pairs.append((y * 8 + x * 2 + c, to_y * 8 + to_x * 2 + c))
    return pairs


def send(array, s, stage):
    return lax.ppermute(array, PLANE, plane_pairs(lambda u: (u + s) % 4, stage))


def exchange(array, bits, stage):
    return lax.ppermute(array, PLANE, plane_pairs(lambda u: u ^ bits, stage))


def on_device(
    hidden,
    group_qkv,
    mlp_branch,
    key_cache,
    paged_value_cache,
    cache_lengths,
    page_table,
    dense_weight,
    dense_bias,
    norm_gain,
    norm_bias,
    qkv_weight,
    qkv_bias,
):
    y = lax.axis_index("y").astype(jnp.int32)
    x = lax.axis_index("x").astype(jnp.int32)
    core = lax.axis_index("core").astype(jnp.int32)
    head = lax.axis_index("head").astype(jnp.int32)
    page = 8 * y + 2 * x + core

    info = jnp.stack([page, y, x, core, head])

    inverse = 1.0 / 10000.0 ** (jnp.arange(0, ROT, 2, dtype=F32) / ROT)
    rates = jnp.broadcast_to(inverse[:, None], (ROT // 2, TOK))
    queries, fresh = rotary(info, cache_lengths, group_qkv, rates)

    other_keys = lax.ppermute(key_cache, "core", CORES)
    other_values = lax.ppermute(paged_value_cache, "core", CORES)
    other_fresh = lax.ppermute(fresh, "core", CORES)
    near = [queries] + [send(queries, s, 0) for s in range(1, 4)]
    codes, counts = page_lists(info, cache_lengths, page_table)
    pool_keys, pool_values = pool(other_keys, other_values)
    neighbour = exchange(fresh, 1, 0)
    near, codes, pool_keys, other_fresh, neighbour = lax.optimization_barrier(
        (near, codes, pool_keys, other_fresh, neighbour)
    )
    near = stack(near)
    all_queries = [near] + [send(near, s, 1) for s in range(1, 4)]

    caches = (key_cache, paged_value_cache, pool_keys, pool_values)

    pair = stack([fresh, neighbour])
    new_rows = stack([pair, exchange(pair, 3, 0)]).reshape(4, TOK, 2 * LW)

    partials = [None] * 4
    last = None
    for s in (0, 1, 3, 2):
        wanted = all_queries[s]
        if last is not None:
            wanted, last = lax.optimization_barrier((wanted, last))
        if s == 1:
            wanted, new_rows = lax.optimization_barrier((wanted, new_rows))
        part = attend(
            s, info, cache_lengths, (codes, counts), wanted, caches, (fresh, other_fresh)
        )
        if last is not None:
            partials[before] = last if before == 0 else send(last, -before, 1)
        last, before = part, s
    partials[before] = send(last, -before, 1)
    from_left = send(new_rows, 1, 1)
    from_right = send(new_rows, 3, 1)
    partials, from_left, from_right = lax.optimization_barrier((partials, from_left, from_right))
    blocks = join_rows(partials)
    blocks, from_left = lax.optimization_barrier((blocks, from_left))
    opposite = send(from_left, 1, 1)
    blocks = [blocks[0]] + [send(blocks[s], -s, 0) for s in range(1, 4)]
    attention = join_last(blocks)

    shares = dense(info, attention, dense_weight, dense_bias, hidden, mlp_branch)
    shares = [shares[0]] + [lax.ppermute(shares[s], "head", shift(s)) for s in range(1, 4)]
    news = [new_rows, from_left, opposite, from_right]
    new_hidden = join_shares(shares)
    news, _ = lax.optimization_barrier((news, new_hidden))
    gathered = stack(news)
    news = (gathered, lax.ppermute(gathered, "core", CORES))

    streams = [new_hidden] + [lax.ppermute(new_hidden, "head", shift(s)) for s in range(1, 4)]
    key_out, value_out, token = patch(
        info, cache_lengths, page_table, news, key_cache, paged_value_cache
    )
    late_weight, _ = lax.optimization_barrier((qkv_weight, new_hidden))
    next_qkv = project_qkv(
        info, token, streams, norm_gain, norm_bias, load(late_weight), qkv_bias
    )

    return (new_hidden, next_qkv, key_out, value_out)


def solution(mesh):
    plane = PLANE
    fine = Mesh(mesh.devices.reshape(4, 4, 4, 2), ("head",) + plane)
    in_specs = (
        P(plane, "head"),
        P(plane, "head"),
        P(plane, "head"),
        P(plane, None, "head"),
        P(plane, None, "head"),
        P(),
        P(),
        P("head", None),
        P(),
        P(),
        P(),
        P(None, "head"),
        P("head"),
    )
    out_specs = (
        P(plane, "head"),
        P(plane, "head"),
        P(plane, None, "head"),
        P(plane, None, "head"),
    )
    return jax.shard_map(
        on_device, mesh=fine, in_specs=in_specs, out_specs=out_specs, check_vma=False
    )
```

```python
import math

import jax
import jax.numpy as jnp
from jax import lax
from jax.experimental import pallas as pl
from jax.experimental.pallas import tpu as pltpu
from jax.sharding import Mesh
from jax.sharding import PartitionSpec as P

D = 4096
HS = 128
ROT = 32
PT = 128
GROUP = 512
LH = 4
LW = LH * HS
SLOTS = 13
REQS = 8
MAXP = 36
TOK = 128
PIECES = LW + 32
COLS = D // 4
QW = 1536
NEG = -1e30
C2 = math.log2(math.e) / math.sqrt(HS)
F32 = jnp.float32
BF16 = jnp.bfloat16
VMEM = pltpu.VMEM
HBM = pltpu.HBM
SMEM = pltpu.SMEM


def whole(space=VMEM):
    return pl.BlockSpec(memory_space=space)


def limit(mib):
    return pltpu.CompilerParams(vmem_limit_bytes=mib << 20)


def head_rows(h):
    return slice(h * HS, (h + 1) * HS)


def rotary_kernel(info, lens, x_ref, rate_ref, q_ref, kv_ref):
    half = ROT // 2
    page = info[0]
    first = lens[lax.div(page, 4)] + lax.rem(page, 4) * TOK
    lane = lax.broadcasted_iota(jnp.int32, (half, TOK), 1)
    angles = (first + lane).astype(F32) * rate_ref[...]
    cosine = jnp.cos(angles)
    sine = jnp.sin(angles)
    for h in range(LH):
        for which in range(2):
            base = (3 * h + which) * HS
            turned = x_ref[:, base : base + HS].astype(F32).T
            a = turned[0:half]
            b = turned[half:ROT]
            done = jnp.concatenate(
                [a * cosine - b * sine, b * cosine + a * sine, turned[ROT:]], axis=0
            )
            if which == 0:
                q_ref[head_rows(h), :] = done.astype(BF16)
            else:
                kv_ref[:, head_rows(h)] = done.T.astype(BF16)
        base = (3 * h + 2) * HS
        kv_ref[:, LW + h * HS : LW + (h + 1) * HS] = x_ref[:, base : base + HS]


def rotary(info, lens, group_qkv, rates):
    return pl.pallas_call(
        rotary_kernel,
        out_shape=(
            jax.ShapeDtypeStruct((LW, TOK), BF16),
            jax.ShapeDtypeStruct((TOK, 2 * LW), BF16),
        ),
        in_specs=[whole(SMEM)] * 2 + [whole()] * 2,
        out_specs=(whole(), whole()),
        compiler_params=limit(2),
        name="rotary",
    )(info, lens, group_qkv, rates)


def stack_kernel(*refs):
    for i, ref in enumerate(refs[:-1]):
        refs[-1][i] = ref[...]


def stack(parts):
    return pl.pallas_call(
        stack_kernel,
        out_shape=jax.ShapeDtypeStruct((len(parts),) + parts[0].shape, parts[0].dtype),
        in_specs=[whole()] * len(parts),
        out_specs=whole(),
        compiler_params=limit(12),
        name="stack",
    )(*parts)


LIST = 32


def list_kernel(info, lens, table, codes, counts):
    core = info[3]
    first_slot = 2 * SLOTS * lax.div(info[0], 2)
    own_first = SLOTS * core

    def scan_request(request, carry):
        length = lens[request]
        found = jnp.int32(0)
        for g in range(LIST):
            slot = table[request, g] - first_slot
            here = (slot >= 0) & (slot < 2 * SLOTS) & (g * PT < length)
            local = slot - own_first
            codes[request, found] = g * LIST + jnp.where(local < 0, local + 2 * SLOTS, local)
            found = found + here.astype(jnp.int32)
        counts[request] = found
        return carry

    lax.fori_loop(0, REQS, scan_request, 0)


def page_lists(info, lens, table):
    return pl.pallas_call(
        list_kernel,
        out_shape=(
            jax.ShapeDtypeStruct((REQS, LIST + 1), jnp.int32),
            jax.ShapeDtypeStruct((REQS,), jnp.int32),
        ),
        in_specs=[whole(SMEM)] * 3,
        out_specs=(whole(SMEM), whole(SMEM)),
        compiler_params=limit(1),
        name="page_lists",
    )(info, lens, table)


def pool_kernel(k_other, v_other, keys, values, sems):
    copies = [
        pltpu.make_async_copy(src.at[i], dst.at[i], sems.at[n, i])
        for n, (src, dst) in enumerate(((k_other, keys), (v_other, values)))
        for i in range(SLOTS)
    ]
    for copy in copies:
        copy.start()
    for copy in copies:
        copy.wait()


def pool(k_other, v_other):
    shape = jax.ShapeDtypeStruct(k_other.shape, BF16)
    return pl.pallas_call(
        pool_kernel,
        out_shape=(shape, shape),
        in_specs=[whole(HBM)] * 2,
        out_specs=(whole(), whole()),
        scratch_shapes=[pltpu.SemaphoreType.DMA((2, SLOTS))],
        compiler_params=limit(8),
        name="pool",
    )(k_other, v_other)


PARTS = 32


def load_kernel(src, dst, sems):
    rows = src.shape[0] // PARTS
    copies = [
        pltpu.make_async_copy(
            src.at[pl.ds(i * rows, rows)], dst.at[pl.ds(i * rows, rows)], sems.at[i]
        )
        for i in range(PARTS)
    ]
    for copy in copies:
        copy.start()
    for copy in copies:
        copy.wait()


def load(array):
    return pl.pallas_call(
        load_kernel,
        out_shape=jax.ShapeDtypeStruct(array.shape, array.dtype),
        in_specs=[whole(HBM)],
        out_specs=whole(),
        scratch_shapes=[pltpu.SemaphoreType.DMA((PARTS,))],
        compiler_params=limit(40),
        name="load",
    )(array)


def split3(value):
    top = value.astype(BF16)
    rest = value - top.astype(F32)
    middle = rest.astype(BF16)
    low = (rest - middle.astype(F32)).astype(BF16)
    return top, middle, low


def stat_rows(stats):
    width = stats.shape[1]
    return jnp.concatenate(
        [piece.astype(F32) for piece in split3(stats)] + [jnp.zeros((8, width), F32)], axis=0
    ).astype(BF16)


def attention_kernel(
    step, info, lens, codes, counts, q_ref, k_own, v_own, k_other, v_other, *rest
):
    if step != 2:
        fresh_own, fresh_other, *rest = rest
    o_ref, acc, stats = rest
    y = info[1]
    x = info[2]
    core = info[3]
    key_row = lax.broadcasted_iota(jnp.int32, (2 * PT, TOK), 0)
    lane = lax.broadcasted_iota(jnp.int32, (2 * PT, TOK), 1)

    def block_loop(block, carry):
        row = lax.bitwise_and(y - jnp.where(core == 0, step, block), 3)
        column = lax.bitwise_and(x - jnp.where(core == 0, block, step), 3)
        request = 2 * row + lax.div(column, 2)

        def absorb(key_of, value_of, mask, guard):
            old = stats[...]
            scores = [
                jnp.where(
                    mask,
                    jnp.dot(key_of(h), q_ref[block, head_rows(h), :], preferred_element_type=F32),
                    NEG,
                )
                for h in range(LH)
            ]
            peaks = [
                jnp.maximum(old[h : h + 1], jnp.max(scores[h], axis=0, keepdims=True))
                for h in range(LH)
            ]
            weights = [jnp.exp2((scores[h] - peaks[h]) * C2) for h in range(LH)]
            if guard:
                weights = [jnp.where(mask, w, 0.0) for w in weights]
            decays = [jnp.exp2((old[h : h + 1] - peaks[h]) * C2) for h in range(LH)]
            totals = [
                old[LH + h : LH + h + 1] * decays[h] + jnp.sum(weights[h], axis=0, keepdims=True)
                for h in range(LH)
            ]
            stats[...] = jnp.concatenate(peaks + totals, axis=0)
            added = [
                lax.dot_general(
                    value_of(h), weights[h].astype(BF16), (((0,), (0,)), ((), ())),
                    preferred_element_type=F32,
                )
                for h in range(LH)
            ]
            for h in range(LH):
                acc[head_rows(h), :] = acc[head_rows(h), :] * decays[h] + added[h]

        acc[...] = jnp.zeros_like(acc)
        stats[...] = jnp.where(lax.broadcasted_iota(jnp.int32, (2 * LH, TOK), 0) < LH, NEG, 0.0)
        count = counts[request]

        def pages_step(i, inner):
            full = 2 * i + 1 < count
            first = codes[request, 2 * i]
            second = codes[request, jnp.where(full, 2 * i + 1, 2 * i)]
            lower = lens[request] - lax.div(first, LIST) * PT
            upper = jnp.where(full, lens[request] - lax.div(second, LIST) * PT, 0) + PT
            mask = key_row < jnp.where(key_row < PT, lower, upper)

            def page_rows(own, other, code, h):
                slot = lax.rem(code, LIST)
                mine = slot < SLOTS
                local = jnp.where(mine, slot, slot - SLOTS)
                return jnp.where(
                    mine, own[local, :, head_rows(h)], other[local, :, head_rows(h)]
                )

            def pair(own, other, h):
                return jnp.concatenate(
                    [page_rows(own, other, first, h), page_rows(own, other, second, h)], axis=0
                )

            absorb(
                lambda h: pair(k_own, k_other, h), lambda h: pair(v_own, v_other, h), mask, False
            )
            return inner

        lax.fori_loop(0, lax.div(count + 1, 2), pages_step, 0)
        if step != 2:

            @pl.when(request == 2 * y + lax.div(x, 2))
            def _():
                pair = lambda cols: jnp.concatenate(
                    [fresh_own[:, cols], fresh_other[:, cols]], axis=0
                )
                token = 2 * lax.bitwise_and(x, 1) * TOK + jnp.where(
                    key_row < PT, key_row + core * TOK, key_row - core * TOK
                )
                query = (2 * lax.bitwise_and(column, 1) + core) * TOK + lane
                absorb(
                    lambda h: pair(head_rows(h)),
                    lambda h: pair(slice(LW + h * HS, LW + (h + 1) * HS)),
                    token <= query,
                    True,
                )

        for h in range(LH):
            o_ref[block, head_rows(h), :] = acc[head_rows(h), :].astype(BF16)
        o_ref[block, LW:PIECES, :] = stat_rows(stats[...])
        return carry

    lax.fori_loop(0, 4, block_loop, 0)


def attend(step, info, lens, lists, queries, caches, fresh):
    operands = [info, lens, *lists, queries, *caches] + ([] if step == 2 else list(fresh))
    specs = [whole(SMEM)] * 4 + [whole()] * (5 if step == 2 else 7)

    def body(*refs):
        attention_kernel(step, *refs)

    return pl.pallas_call(
        body,
        out_shape=jax.ShapeDtypeStruct((4, PIECES, TOK), BF16),
        in_specs=specs,
        out_specs=whole(),
        scratch_shapes=[VMEM((LW, TOK), F32), VMEM((2 * LH, TOK), F32)],
        compiler_params=limit(12),
        cost_estimate=pl.CostEstimate(flops=0, transcendentals=0, bytes_accessed=0),
        name="attend%d" % step,
    )(*operands)


def join(parts):
    read = []
    for part in parts:
        tail = part[LW:PIECES].astype(F32)
        read.append(tail[0:8] + tail[8:16] + tail[16:24])
    peak = read[0][0:LH]
    for value in read[1:]:
        peak = jnp.maximum(peak, value[0:LH])
    factors = [jnp.exp2((value[0:LH] - peak) * C2) for value in read]
    total = sum(value[LH : 2 * LH] * factor for value, factor in zip(read, factors))
    weighted = [
        sum(
            part[head_rows(h)].astype(F32) * factor[h : h + 1]
            for part, factor in zip(parts, factors)
        )
        for h in range(LH)
    ]
    return peak, total, weighted


def join_rows_kernel(a_ref, b_ref, c_ref, d_ref, *outs):
    for block, out in enumerate(outs):
        parts = [ref.at[block] for ref in (a_ref, b_ref, c_ref, d_ref)]
        peak, total, weighted = join(parts)
        for h in range(LH):
            out[head_rows(h), :] = weighted[h].astype(BF16)
        out[LW:PIECES, :] = stat_rows(jnp.concatenate([peak, total], axis=0))


def join_last_kernel(a_ref, b_ref, c_ref, d_ref, out):
    _, total, weighted = join([a_ref, b_ref, c_ref, d_ref])
    inverse = 1.0 / total
    for h in range(LH):
        out[:, head_rows(h)] = (weighted[h] * inverse[h : h + 1]).T.astype(BF16)


def join_rows(parts):
    return pl.pallas_call(
        join_rows_kernel,
        out_shape=tuple(jax.ShapeDtypeStruct((PIECES, TOK), BF16) for _ in range(4)),
        in_specs=[whole()] * 4,
        out_specs=tuple(whole() for _ in range(4)),
        compiler_params=limit(8),
        name="join_rows",
    )(*parts)


def join_last(parts):
    return pl.pallas_call(
        join_last_kernel,
        out_shape=jax.ShapeDtypeStruct((TOK, LW), BF16),
        in_specs=[whole()] * 4,
        out_specs=whole(),
        compiler_params=limit(4),
        name="join_last",
    )(*parts)


def dense_kernel(info, attention, weight, bias, hidden, branch, own, *outs):
    head = info[4]
    base = pl.ds(pl.multiple_of(head * COLS, COLS), COLS)
    for s in range(4):
        target = lax.bitwise_and(head + s, 3)
        cols = pl.ds(pl.multiple_of(target * COLS, COLS), COLS)
        product = jnp.dot(attention[...], weight[:, cols], preferred_element_type=F32)
        if s == 0:
            rest = bias[base].reshape(1, COLS) + hidden[...].astype(F32) + branch[...].astype(F32)
            own[...] = product + rest
        else:
            outs[s - 1][...] = product.astype(BF16)


def dense(info, attention, weight, bias, hidden, branch):
    shape = jax.ShapeDtypeStruct((TOK, COLS), BF16)
    return pl.pallas_call(
        dense_kernel,
        out_shape=(jax.ShapeDtypeStruct((TOK, COLS), F32), shape, shape, shape),
        in_specs=[whole(SMEM)] + [whole()] * 5,
        out_specs=(whole(),) * 4,
        compiler_params=limit(10),
        name="dense",
    )(info, attention, weight, bias, hidden, branch)


def join_shares_kernel(own, a, b, c, out):
    out[...] = (
        own[...] + (a[...].astype(F32) + b[...].astype(F32) + c[...].astype(F32))
    ).astype(BF16)


def join_shares(parts):
    return pl.pallas_call(
        join_shares_kernel,
        out_shape=jax.ShapeDtypeStruct((TOK, COLS), BF16),
        in_specs=[whole()] * 4,
        out_specs=whole(),
        compiler_params=limit(4),
        name="join_shares",
    )(*parts)


def qkv_kernel(info, token, x0, x1, x2, x3, gain, shift, weight, bias, out):
    head = info[4]
    blocks = (x0, x1, x2, x3)
    total = 0.0
    square = 0.0
    for block in blocks:
        value = block[...].astype(F32)
        total = total + jnp.sum(value, axis=1, keepdims=True)
        square = square + jnp.sum(value * value, axis=1, keepdims=True)
    mean = total / D
    variance = square / D - mean * mean
    scale = lax.rsqrt(variance + 1e-05)
    result = bias[...].reshape(1, QW) + jnp.zeros((TOK, QW), F32)
    for s, block in enumerate(blocks):
        origin = lax.bitwise_and(head - s, 3)
        rows = pl.ds(pl.multiple_of(origin * COLS, COLS), COLS)
        normed = (block[...].astype(F32) - mean) * scale * gain[rows].reshape(1, COLS)
        normed = (normed + shift[rows].reshape(1, COLS)).astype(BF16)
        result = result + jnp.dot(normed, weight[rows, :], preferred_element_type=F32)
    out[...] = result.astype(BF16)


def project_qkv(info, token, blocks, gain, shift, weight, bias):
    return pl.pallas_call(
        qkv_kernel,
        out_shape=jax.ShapeDtypeStruct((TOK, QW), BF16),
        in_specs=[whole(SMEM)] * 2 + [whole()] * 8,
        out_specs=whole(),
        compiler_params=limit(20),
        name="project_qkv",
    )(info, token, *blocks, gain, shift, weight, bias)


WINDOW = 2 * TOK


def patch_kernel(info, lens, table, *refs):
    news = refs[0:2]
    k_in, v_in, k_out, v_out, token_out, src, kbuf, vbuf, sems, bulk, slots, offsets = refs[2:]
    page = info[0]
    y = info[1]
    x = info[2]
    core = info[3]
    whole_copies = (
        pltpu.make_async_copy(k_in, k_out, bulk.at[0]),
        pltpu.make_async_copy(v_in, v_out, bulk.at[1]),
    )
    for copy in whole_copies:
        copy.start()

    def source(n, half, ref, outer, inner):
        return pltpu.make_async_copy(
            ref.at[outer, inner], src.at[n, pl.ds(half * TOK, TOK), :], sems.at[n, half]
        )

    def loads(n, local):
        return (
            pltpu.make_async_copy(k_in.at[local], kbuf.at[n], sems.at[n, 2]),
            pltpu.make_async_copy(v_in.at[local], vbuf.at[n], sems.at[n, 3]),
        )

    def stores(n, local):
        return (
            pltpu.make_async_copy(kbuf.at[n], k_out.at[local], sems.at[n, 4]),
            pltpu.make_async_copy(vbuf.at[n], v_out.at[local], sems.at[n, 5]),
        )

    def scan_request(request, count):
        length = lens[request]
        first = lax.div(length, PT)
        last = lax.div(length + (GROUP - 1), PT)

        def scan(g, n):
            slot = table[request, g]
            here = lax.div(slot, SLOTS) == page

            @pl.when(here)
            def _():
                local = slot - page * SLOTS
                offset = g * PT - length
                lower = lax.div(offset + PT, PT) - 1
                slots[n] = local
                offsets[n] = offset
                for copy in loads(n, local):
                    copy.start()
                row = lax.div(request, 2)
                for half in range(2):
                    block = jnp.clip(lower + half, 0, 3)
                    column = 2 * lax.rem(request, 2) + lax.div(block, 2)
                    origin = lax.rem(block, 2)
                    inner = jnp.where(origin == 0, column ^ x, row ^ y)
                    inner = inner ^ lax.div(inner, 2)
                    outer = lax.bitwise_and(jnp.where(origin == 0, y - row, x - column), 3)

                    @pl.when(origin == core)
                    def _(half=half, outer=outer, inner=inner):
                        source(n, half, news[0], outer, inner).start()

                    @pl.when(origin != core)
                    def _(half=half, outer=outer, inner=inner):
                        source(n, half, news[1], outer, inner).start()

            return n + here.astype(jnp.int32)

        return lax.fori_loop(first, last + 1, scan, count)

    count = lax.fori_loop(0, REQS, scan_request, jnp.int32(0))
    token_out[0] = count
    pick_row = lax.broadcasted_iota(jnp.int32, (PT, WINDOW), 0)
    pick_col = lax.broadcasted_iota(jnp.int32, (PT, WINDOW), 1)
    token = lax.broadcasted_iota(jnp.int32, (PT, LW), 0)

    def update(n, carry):
        for half in range(2):
            source(n, half, news[0], 0, 0).wait()
        for copy in loads(n, 0):
            copy.wait()
        offset = offsets[n]
        base = (lax.div(offset + PT, PT) - 1) * PT
        pick = jnp.where(pick_col == pick_row + (offset - base), 1.0, 0.0).astype(BF16)
        index = token + offset
        fresh = (index >= 0) & (index < GROUP)
        for buf, cols in ((kbuf, slice(0, LW)), (vbuf, slice(LW, 2 * LW))):
            moved = jnp.dot(pick, src[n, :, cols], preferred_element_type=F32)
            buf[n] = jnp.where(fresh, moved, buf[n].astype(F32)).astype(BF16)
        return carry

    def put(n, carry):
        for copy in stores(n, slots[n]):
            copy.start()
        return carry

    def finish(n, carry):
        for copy in stores(n, 0):
            copy.wait()
        return carry

    lax.fori_loop(0, count, update, 0)
    for copy in whole_copies:
        copy.wait()
    lax.fori_loop(0, count, put, 0)
    lax.fori_loop(0, count, finish, 0)


def patch(info, lens, table, news, key_cache, value_cache):
    shape = jax.ShapeDtypeStruct(key_cache.shape, BF16)
    return pl.pallas_call(
        patch_kernel,
        out_shape=(shape, shape, jax.ShapeDtypeStruct((1,), jnp.int32)),
        in_specs=[whole(SMEM)] * 3 + [whole(HBM)] * 4,
        out_specs=(whole(HBM), whole(HBM), whole(SMEM)),
        scratch_shapes=[
            VMEM((SLOTS, WINDOW, 2 * LW), BF16),
            VMEM((SLOTS, PT, LW), BF16),
            VMEM((SLOTS, PT, LW), BF16),
            pltpu.SemaphoreType.DMA((SLOTS, 6)),
            pltpu.SemaphoreType.DMA((2,)),
            SMEM((SLOTS,), jnp.int32),
            SMEM((SLOTS,), jnp.int32),
        ],
        compiler_params=pltpu.CompilerParams(vmem_limit_bytes=20 << 20),
        name="patch",
    )(info, lens, table, *news, key_cache, value_cache)


def shift(s):
    return [(i, (i + s) % 4) for i in range(4)]


PLANE = ("y", "x", "core")
CORES = [(0, 1), (1, 0)]


def plane_pairs(target, stage):
    pairs = []
    for y in range(4):
        for x in range(4):
            for c in range(2):
                along_x = (c == 0) == (stage == 0)
                to_y, to_x = (y, target(x)) if along_x else (target(y), x)
                pairs.append((y * 8 + x * 2 + c, to_y * 8 + to_x * 2 + c))
    return pairs


def send(array, s, stage):
    return lax.ppermute(array, PLANE, plane_pairs(lambda u: (u + s) % 4, stage))


def exchange(array, bits, stage):
    return lax.ppermute(array, PLANE, plane_pairs(lambda u: u ^ bits, stage))


def on_device(
    hidden,
    group_qkv,
    mlp_branch,
    key_cache,
    paged_value_cache,
    cache_lengths,
    page_table,
    dense_weight,
    dense_bias,
    norm_gain,
    norm_bias,
    qkv_weight,
    qkv_bias,
):
    y = lax.axis_index("y").astype(jnp.int32)
    x = lax.axis_index("x").astype(jnp.int32)
    core = lax.axis_index("core").astype(jnp.int32)
    head = lax.axis_index("head").astype(jnp.int32)
    page = 8 * y + 2 * x + core

    info = jnp.stack([page, y, x, core, head])

    inverse = 1.0 / 10000.0 ** (jnp.arange(0, ROT, 2, dtype=F32) / ROT)
    rates = jnp.broadcast_to(inverse[:, None], (ROT // 2, TOK))
    queries, fresh = rotary(info, cache_lengths, group_qkv, rates)

    other_keys = lax.ppermute(key_cache, "core", CORES)
    other_values = lax.ppermute(paged_value_cache, "core", CORES)
    other_fresh = lax.ppermute(fresh, "core", CORES)
    near = [queries] + [send(queries, s, 0) for s in range(1, 4)]
    codes, counts = page_lists(info, cache_lengths, page_table)
    pool_keys, pool_values = pool(other_keys, other_values)
    neighbour = exchange(fresh, 1, 0)
    near, codes, pool_keys, other_fresh, neighbour = lax.optimization_barrier(
        (near, codes, pool_keys, other_fresh, neighbour)
    )
    near = stack(near)
    all_queries = [near] + [send(near, s, 1) for s in range(1, 4)]

    caches = (key_cache, paged_value_cache, pool_keys, pool_values)

    pair = stack([fresh, neighbour])

    partials = [None] * 4
    last = None
    for s in (0, 1, 3, 2):
        wanted = all_queries[s]
        if last is not None:
            wanted, last = lax.optimization_barrier((wanted, last))
        if s == 1:
            wanted, pair = lax.optimization_barrier((wanted, pair))
            new_rows = stack([pair, exchange(pair, 3, 0)]).reshape(4, TOK, 2 * LW)
        if s == 2:
            wanted, new_rows = lax.optimization_barrier((wanted, new_rows))
        part = attend(
            s, info, cache_lengths, (codes, counts), wanted, caches, (fresh, other_fresh)
        )
        if last is not None:
            partials[before] = last if before == 0 else send(last, -before, 1)
        last, before = part, s
    partials[before] = send(last, -before, 1)
    blocks = join_rows(partials)
    blocks, new_rows = lax.optimization_barrier((blocks, new_rows))
    from_left = send(new_rows, 1, 1)
    from_right = send(new_rows, 3, 1)
    blocks = [blocks[0]] + [send(blocks[s], -s, 0) for s in range(1, 4)]
    attention = join_last(blocks)

    shares = dense(info, attention, dense_weight, dense_bias, hidden, mlp_branch)
    shares = [shares[0]] + [lax.ppermute(shares[s], "head", shift(s)) for s in range(1, 4)]
    from_left, from_right, _ = lax.optimization_barrier((from_left, from_right, shares[0]))
    opposite = send(from_left, 1, 1)
    news = [new_rows, from_left, opposite, from_right]
    new_hidden = join_shares(shares)
    news, _ = lax.optimization_barrier((news, new_hidden))
    gathered = stack(news)
    news = (gathered, lax.ppermute(gathered, "core", CORES))

    streams = [new_hidden] + [lax.ppermute(new_hidden, "head", shift(s)) for s in range(1, 4)]
    key_out, value_out, token = patch(
        info, cache_lengths, page_table, news, key_cache, paged_value_cache
    )
    late_weight, _ = lax.optimization_barrier((qkv_weight, new_hidden))
    next_qkv = project_qkv(
        info, token, streams, norm_gain, norm_bias, load(late_weight), qkv_bias
    )

    return (new_hidden, next_qkv, key_out, value_out)


def solution(mesh):
    plane = PLANE
    fine = Mesh(mesh.devices.reshape(4, 4, 4, 2), ("head",) + plane)
    in_specs = (
        P(plane, "head"),
        P(plane, "head"),
        P(plane, "head"),
        P(plane, None, "head"),
        P(plane, None, "head"),
        P(),
        P(),
        P("head", None),
        P(),
        P(),
        P(),
        P(None, "head"),
        P("head"),
    )
    out_specs = (
        P(plane, "head"),
        P(plane, "head"),
        P(plane, None, "head"),
        P(plane, None, "head"),
    )
    return jax.shard_map(
        on_device, mesh=fine, in_specs=in_specs, out_specs=out_specs, check_vma=False
    )
```

```python
import math

import jax
import jax.numpy as jnp
from jax import lax
from jax.experimental import pallas as pl
from jax.experimental.pallas import tpu as pltpu
from jax.sharding import Mesh
from jax.sharding import PartitionSpec as P

D = 4096
HS = 128
ROT = 32
PT = 128
GROUP = 512
LH = 4
LW = LH * HS
SLOTS = 13
REQS = 8
MAXP = 36
TOK = 128
PIECES = LW + 32
COLS = D // 4
QW = 1536
NEG = -1e30
C2 = math.log2(math.e) / math.sqrt(HS)
F32 = jnp.float32
BF16 = jnp.bfloat16
VMEM = pltpu.VMEM
HBM = pltpu.HBM
SMEM = pltpu.SMEM


def whole(space=VMEM):
    return pl.BlockSpec(memory_space=space)


def limit(mib):
    return pltpu.CompilerParams(vmem_limit_bytes=mib << 20)


def head_rows(h):
    return slice(h * HS, (h + 1) * HS)


def rotary_kernel(info, lens, x_ref, rate_ref, q_ref, kv_ref):
    half = ROT // 2
    page = info[0]
    first = lens[lax.div(page, 4)] + lax.rem(page, 4) * TOK
    lane = lax.broadcasted_iota(jnp.int32, (half, TOK), 1)
    angles = (first + lane).astype(F32) * rate_ref[...]
    cosine = jnp.cos(angles)
    sine = jnp.sin(angles)
    for h in range(LH):
        for which in range(2):
            base = (3 * h + which) * HS
            turned = x_ref[:, base : base + HS].astype(F32).T
            a = turned[0:half]
            b = turned[half:ROT]
            done = jnp.concatenate(
                [a * cosine - b * sine, b * cosine + a * sine, turned[ROT:]], axis=0
            )
            if which == 0:
                q_ref[head_rows(h), :] = done.astype(BF16)
            else:
                kv_ref[:, head_rows(h)] = done.T.astype(BF16)
        base = (3 * h + 2) * HS
        kv_ref[:, LW + h * HS : LW + (h + 1) * HS] = x_ref[:, base : base + HS]


def rotary(info, lens, group_qkv, rates):
    return pl.pallas_call(
        rotary_kernel,
        out_shape=(
            jax.ShapeDtypeStruct((LW, TOK), BF16),
            jax.ShapeDtypeStruct((TOK, 2 * LW), BF16),
        ),
        in_specs=[whole(SMEM)] * 2 + [whole()] * 2,
        out_specs=(whole(), whole()),
        compiler_params=limit(2),
        name="rotary",
    )(info, lens, group_qkv, rates)


def stack_kernel(*refs):
    for i, ref in enumerate(refs[:-1]):
        refs[-1][i] = ref[...]


def stack(parts):
    return pl.pallas_call(
        stack_kernel,
        out_shape=jax.ShapeDtypeStruct((len(parts),) + parts[0].shape, parts[0].dtype),
        in_specs=[whole()] * len(parts),
        out_specs=whole(),
        compiler_params=limit(12),
        name="stack",
    )(*parts)


LIST = 32


def list_kernel(info, lens, table, codes, counts):
    core = info[3]
    first_slot = 2 * SLOTS * lax.div(info[0], 2)
    own_first = SLOTS * core

    def scan_request(request, carry):
        length = lens[request]
        found = jnp.int32(0)
        for g in range(LIST):
            slot = table[request, g] - first_slot
            here = (slot >= 0) & (slot < 2 * SLOTS) & (g * PT < length)
            local = slot - own_first
            codes[request, found] = g * LIST + jnp.where(local < 0, local + 2 * SLOTS, local)
            found = found + here.astype(jnp.int32)
        counts[request] = found
        return carry

    lax.fori_loop(0, REQS, scan_request, 0)


def page_lists(info, lens, table):
    return pl.pallas_call(
        list_kernel,
        out_shape=(
            jax.ShapeDtypeStruct((REQS, LIST + 1), jnp.int32),
            jax.ShapeDtypeStruct((REQS,), jnp.int32),
        ),
        in_specs=[whole(SMEM)] * 3,
        out_specs=(whole(SMEM), whole(SMEM)),
        compiler_params=limit(1),
        name="page_lists",
    )(info, lens, table)


def pool_kernel(k_other, v_other, keys, values, sems):
    copies = [
        pltpu.make_async_copy(src.at[i], dst.at[i], sems.at[n, i])
        for n, (src, dst) in enumerate(((k_other, keys), (v_other, values)))
        for i in range(SLOTS)
    ]
    for copy in copies:
        copy.start()
    for copy in copies:
        copy.wait()


def pool(k_other, v_other):
    shape = jax.ShapeDtypeStruct(k_other.shape, BF16)
    return pl.pallas_call(
        pool_kernel,
        out_shape=(shape, shape),
        in_specs=[whole(HBM)] * 2,
        out_specs=(whole(), whole()),
        scratch_shapes=[pltpu.SemaphoreType.DMA((2, SLOTS))],
        compiler_params=limit(8),
        name="pool",
    )(k_other, v_other)


PARTS = 32


def load_kernel(src, dst, sems):
    rows = src.shape[0] // PARTS
    copies = [
        pltpu.make_async_copy(
            src.at[pl.ds(i * rows, rows)], dst.at[pl.ds(i * rows, rows)], sems.at[i]
        )
        for i in range(PARTS)
    ]
    for copy in copies:
        copy.start()
    for copy in copies:
        copy.wait()


def load(array):
    return pl.pallas_call(
        load_kernel,
        out_shape=jax.ShapeDtypeStruct(array.shape, array.dtype),
        in_specs=[whole(HBM)],
        out_specs=whole(),
        scratch_shapes=[pltpu.SemaphoreType.DMA((PARTS,))],
        compiler_params=limit(40),
        name="load",
    )(array)


def split3(value):
    top = value.astype(BF16)
    rest = value - top.astype(F32)
    middle = rest.astype(BF16)
    low = (rest - middle.astype(F32)).astype(BF16)
    return top, middle, low


def stat_rows(stats):
    width = stats.shape[1]
    return jnp.concatenate(
        [piece.astype(F32) for piece in split3(stats)] + [jnp.zeros((8, width), F32)], axis=0
    ).astype(BF16)


def attention_kernel(
    step, info, lens, codes, counts, q_ref, k_own, v_own, k_other, v_other, *rest
):
    if step != 2:
        fresh_own, fresh_other, *rest = rest
    o_ref, acc, stats = rest
    y = info[1]
    x = info[2]
    core = info[3]
    key_row = lax.broadcasted_iota(jnp.int32, (2 * PT, TOK), 0)
    lane = lax.broadcasted_iota(jnp.int32, (2 * PT, TOK), 1)

    def absorb(sides):
        work = [(side, h) for side in sides for h in range(LH)]
        old = {side[0]: stats[side[0]] for side in sides}
        scores = [
            jnp.where(
                side[4],
                jnp.dot(
                    side[2](h), q_ref[side[1], head_rows(h), :], preferred_element_type=F32
                ),
                NEG,
            )
            for side, h in work
        ]
        peaks = [
            jnp.maximum(old[side[0]][h : h + 1], jnp.max(score, axis=0, keepdims=True))
            for (side, h), score in zip(work, scores)
        ]
        weights = [
            jnp.where(side[4], jnp.exp2((score - peak) * C2), 0.0)
            for (side, h), score, peak in zip(work, scores, peaks)
        ]
        decays = [
            jnp.exp2((old[side[0]][h : h + 1] - peak) * C2)
            for (side, h), peak in zip(work, peaks)
        ]
        totals = [
            old[side[0]][LH + h : LH + h + 1] * decay + jnp.sum(weight, axis=0, keepdims=True)
            for (side, h), decay, weight in zip(work, decays, weights)
        ]
        for n, side in enumerate(sides):
            rows = slice(n * LH, (n + 1) * LH)
            stats[side[0]] = jnp.concatenate(peaks[rows] + totals[rows], axis=0)
        added = [
            lax.dot_general(
                side[3](h), weight.astype(BF16), (((0,), (0,)), ((), ())),
                preferred_element_type=F32,
            )
            for (side, h), weight in zip(work, weights)
        ]
        for (side, h), decay, add in zip(work, decays, added):
            acc[side[0], head_rows(h), :] = acc[side[0], head_rows(h), :] * decay + add

    straight = (core == 0) & (lax.bitwise_and(x, 1) == 1)

    def pair_loop(j, carry):
        blocks = (jnp.where(straight, 2 * j, j), jnp.where(straight, 2 * j + 1, 3 - j))
        rows = [lax.bitwise_and(y - jnp.where(core == 0, step, block), 3) for block in blocks]
        columns = [lax.bitwise_and(x - jnp.where(core == 0, block, step), 3) for block in blocks]
        requests = [2 * row + lax.div(column, 2) for row, column in zip(rows, columns)]
        amounts = [counts[request] for request in requests]
        acc[...] = jnp.zeros_like(acc)
        start = jnp.where(lax.broadcasted_iota(jnp.int32, (2 * LH, TOK), 0) < LH, NEG, 0.0)
        stats[0] = start
        stats[1] = start

        def pages_step(i, inner):
            sides = []
            for t in range(2):
                request, amount = requests[t], amounts[t]
                first = codes[request, jnp.maximum(jnp.minimum(2 * i, amount - 1), 0)]
                second = codes[request, jnp.maximum(jnp.minimum(2 * i + 1, amount - 1), 0)]
                first = jnp.where(amount > 0, first, 0)
                second = jnp.where(amount > 0, second, 0)
                lower = jnp.where(
                    2 * i < amount, lens[request] - lax.div(first, LIST) * PT, 0
                )
                upper = jnp.where(
                    2 * i + 1 < amount, lens[request] - lax.div(second, LIST) * PT, 0
                )
                mask = key_row < jnp.where(key_row < PT, lower, upper + PT)

                def page_rows(own, other, code, h):
                    slot = lax.rem(code, LIST)
                    mine = slot < SLOTS
                    local = jnp.where(mine, slot, slot - SLOTS)
                    return jnp.where(
                        mine, own[local, :, head_rows(h)], other[local, :, head_rows(h)]
                    )

                def both(own, other, h, first=first, second=second):
                    return jnp.concatenate(
                        [page_rows(own, other, first, h), page_rows(own, other, second, h)],
                        axis=0,
                    )

                sides.append(
                    (
                        t,
                        blocks[t],
                        lambda h, both=both: both(k_own, k_other, h),
                        lambda h, both=both: both(v_own, v_other, h),
                        mask,
                    )
                )
            absorb(sides)
            return inner

        most = jnp.maximum(amounts[0], amounts[1])
        lax.fori_loop(0, lax.div(most + 1, 2), pages_step, 0)
        if step != 2:
            for t in range(2):

                @pl.when(requests[t] == 2 * y + lax.div(x, 2))
                def _(t=t):
                    both = lambda cols: jnp.concatenate(
                        [fresh_own[:, cols], fresh_other[:, cols]], axis=0
                    )
                    token = 2 * lax.bitwise_and(x, 1) * TOK + jnp.where(
                        key_row < PT, key_row + core * TOK, key_row - core * TOK
                    )
                    query = (2 * lax.bitwise_and(columns[t], 1) + core) * TOK + lane
                    absorb(
                        [
                            (
                                t,
                                blocks[t],
                                lambda h: both(head_rows(h)),
                                lambda h: both(slice(LW + h * HS, LW + (h + 1) * HS)),
                                token <= query,
                            )
                        ]
                    )

        for t in range(2):
            for h in range(LH):
                o_ref[blocks[t], head_rows(h), :] = acc[t, head_rows(h), :].astype(BF16)
            o_ref[blocks[t], LW:PIECES, :] = stat_rows(stats[t])
        return carry

    lax.fori_loop(0, 2, pair_loop, 0)


def attend(step, info, lens, lists, queries, caches, fresh):
    operands = [info, lens, *lists, queries, *caches] + ([] if step == 2 else list(fresh))
    specs = [whole(SMEM)] * 4 + [whole()] * (5 if step == 2 else 7)

    def body(*refs):
        attention_kernel(step, *refs)

    return pl.pallas_call(
        body,
        out_shape=jax.ShapeDtypeStruct((4, PIECES, TOK), BF16),
        in_specs=specs,
        out_specs=whole(),
        scratch_shapes=[VMEM((2, LW, TOK), F32), VMEM((2, 2 * LH, TOK), F32)],
        compiler_params=limit(12),
        cost_estimate=pl.CostEstimate(flops=0, transcendentals=0, bytes_accessed=0),
        name="attend%d" % step,
    )(*operands)


def join(parts):
    read = []
    for part in parts:
        tail = part[LW:PIECES].astype(F32)
        read.append(tail[0:8] + tail[8:16] + tail[16:24])
    peak = read[0][0:LH]
    for value in read[1:]:
        peak = jnp.maximum(peak, value[0:LH])
    factors = [jnp.exp2((value[0:LH] - peak) * C2) for value in read]
    total = sum(value[LH : 2 * LH] * factor for value, factor in zip(read, factors))
    weighted = [
        sum(
            part[head_rows(h)].astype(F32) * factor[h : h + 1]
            for part, factor in zip(parts, factors)
        )
        for h in range(LH)
    ]
    return peak, total, weighted


def join_rows_kernel(a_ref, b_ref, c_ref, d_ref, *outs):
    for block, out in enumerate(outs):
        parts = [ref.at[block] for ref in (a_ref, b_ref, c_ref, d_ref)]
        peak, total, weighted = join(parts)
        for h in range(LH):
            out[head_rows(h), :] = weighted[h].astype(BF16)
        out[LW:PIECES, :] = stat_rows(jnp.concatenate([peak, total], axis=0))


def join_last_kernel(a_ref, b_ref, c_ref, d_ref, out):
    _, total, weighted = join([a_ref, b_ref, c_ref, d_ref])
    inverse = 1.0 / total
    for h in range(LH):
        out[:, head_rows(h)] = (weighted[h] * inverse[h : h + 1]).T.astype(BF16)


def join_rows(parts):
    return pl.pallas_call(
        join_rows_kernel,
        out_shape=tuple(jax.ShapeDtypeStruct((PIECES, TOK), BF16) for _ in range(4)),
        in_specs=[whole()] * 4,
        out_specs=tuple(whole() for _ in range(4)),
        compiler_params=limit(8),
        name="join_rows",
    )(*parts)


def join_last(parts):
    return pl.pallas_call(
        join_last_kernel,
        out_shape=jax.ShapeDtypeStruct((TOK, LW), BF16),
        in_specs=[whole()] * 4,
        out_specs=whole(),
        compiler_params=limit(4),
        name="join_last",
    )(*parts)


def dense_kernel(info, attention, weight, bias, hidden, branch, own, *outs):
    head = info[4]
    base = pl.ds(pl.multiple_of(head * COLS, COLS), COLS)
    for s in range(4):
        target = lax.bitwise_and(head + s, 3)
        cols = pl.ds(pl.multiple_of(target * COLS, COLS), COLS)
        product = jnp.dot(attention[...], weight[:, cols], preferred_element_type=F32)
        if s == 0:
            rest = bias[base].reshape(1, COLS) + hidden[...].astype(F32) + branch[...].astype(F32)
            own[...] = product + rest
        else:
            outs[s - 1][...] = product.astype(BF16)


def dense(info, attention, weight, bias, hidden, branch):
    shape = jax.ShapeDtypeStruct((TOK, COLS), BF16)
    return pl.pallas_call(
        dense_kernel,
        out_shape=(jax.ShapeDtypeStruct((TOK, COLS), F32), shape, shape, shape),
        in_specs=[whole(SMEM)] + [whole()] * 5,
        out_specs=(whole(),) * 4,
        compiler_params=limit(10),
        name="dense",
    )(info, attention, weight, bias, hidden, branch)


def join_shares_kernel(own, a, b, c, out):
    out[...] = (
        own[...] + (a[...].astype(F32) + b[...].astype(F32) + c[...].astype(F32))
    ).astype(BF16)


def join_shares(parts):
    return pl.pallas_call(
        join_shares_kernel,
        out_shape=jax.ShapeDtypeStruct((TOK, COLS), BF16),
        in_specs=[whole()] * 4,
        out_specs=whole(),
        compiler_params=limit(4),
        name="join_shares",
    )(*parts)


def qkv_kernel(info, token, x0, x1, x2, x3, gain, shift, weight, bias, out):
    head = info[4]
    blocks = (x0, x1, x2, x3)
    total = 0.0
    square = 0.0
    for block in blocks:
        value = block[...].astype(F32)
        total = total + jnp.sum(value, axis=1, keepdims=True)
        square = square + jnp.sum(value * value, axis=1, keepdims=True)
    mean = total / D
    variance = square / D - mean * mean
    scale = lax.rsqrt(variance + 1e-05)
    result = bias[...].reshape(1, QW) + jnp.zeros((TOK, QW), F32)
    for s, block in enumerate(blocks):
        origin = lax.bitwise_and(head - s, 3)
        rows = pl.ds(pl.multiple_of(origin * COLS, COLS), COLS)
        normed = (block[...].astype(F32) - mean) * scale * gain[rows].reshape(1, COLS)
        normed = (normed + shift[rows].reshape(1, COLS)).astype(BF16)
        result = result + jnp.dot(normed, weight[rows, :], preferred_element_type=F32)
    out[...] = result.astype(BF16)


def project_qkv(info, token, blocks, gain, shift, weight, bias):
    return pl.pallas_call(
        qkv_kernel,
        out_shape=jax.ShapeDtypeStruct((TOK, QW), BF16),
        in_specs=[whole(SMEM)] * 2 + [whole()] * 8,
        out_specs=whole(),
        compiler_params=limit(20),
        name="project_qkv",
    )(info, token, *blocks, gain, shift, weight, bias)


WINDOW = 2 * TOK


def patch_kernel(info, lens, table, *refs):
    news = refs[0:2]
    k_in, v_in, k_out, v_out, token_out, src, kbuf, vbuf, sems, bulk, slots, offsets = refs[2:]
    page = info[0]
    y = info[1]
    x = info[2]
    core = info[3]
    whole_copies = (
        pltpu.make_async_copy(k_in, k_out, bulk.at[0]),
        pltpu.make_async_copy(v_in, v_out, bulk.at[1]),
    )
    for copy in whole_copies:
        copy.start()

    def source(n, half, ref, outer, inner):
        return pltpu.make_async_copy(
            ref.at[outer, inner], src.at[n, pl.ds(half * TOK, TOK), :], sems.at[n, half]
        )

    def loads(n, local):
        return (
            pltpu.make_async_copy(k_in.at[local], kbuf.at[n], sems.at[n, 2]),
            pltpu.make_async_copy(v_in.at[local], vbuf.at[n], sems.at[n, 3]),
        )

    def stores(n, local):
        return (
            pltpu.make_async_copy(kbuf.at[n], k_out.at[local], sems.at[n, 4]),
            pltpu.make_async_copy(vbuf.at[n], v_out.at[local], sems.at[n, 5]),
        )

    def scan_request(request, count):
        length = lens[request]
        first = lax.div(length, PT)
        last = lax.div(length + (GROUP - 1), PT)

        def scan(g, n):
            slot = table[request, g]
            here = lax.div(slot, SLOTS) == page

            @pl.when(here)
            def _():
                local = slot - page * SLOTS
                offset = g * PT - length
                lower = lax.div(offset + PT, PT) - 1
                slots[n] = local
                offsets[n] = offset
                for copy in loads(n, local):
                    copy.start()
                row = lax.div(request, 2)
                for half in range(2):
                    block = jnp.clip(lower + half, 0, 3)
                    column = 2 * lax.rem(request, 2) + lax.div(block, 2)
                    origin = lax.rem(block, 2)
                    inner = jnp.where(origin == 0, column ^ x, row ^ y)
                    inner = inner ^ lax.div(inner, 2)
                    outer = lax.bitwise_and(jnp.where(origin == 0, y - row, x - column), 3)

                    @pl.when(origin == core)
                    def _(half=half, outer=outer, inner=inner):
                        source(n, half, news[0], outer, inner).start()

                    @pl.when(origin != core)
                    def _(half=half, outer=outer, inner=inner):
                        source(n, half, news[1], outer, inner).start()

            return n + here.astype(jnp.int32)

        return lax.fori_loop(first, last + 1, scan, count)

    count = lax.fori_loop(0, REQS, scan_request, jnp.int32(0))
    token_out[0] = count
    pick_row = lax.broadcasted_iota(jnp.int32, (PT, WINDOW), 0)
    pick_col = lax.broadcasted_iota(jnp.int32, (PT, WINDOW), 1)
    token = lax.broadcasted_iota(jnp.int32, (PT, LW), 0)

    def update(n, carry):
        for half in range(2):
            source(n, half, news[0], 0, 0).wait()
        for copy in loads(n, 0):
            copy.wait()
        offset = offsets[n]
        base = (lax.div(offset + PT, PT) - 1) * PT
        pick = jnp.where(pick_col == pick_row + (offset - base), 1.0, 0.0).astype(BF16)
        index = token + offset
        fresh = (index >= 0) & (index < GROUP)
        for buf, cols in ((kbuf, slice(0, LW)), (vbuf, slice(LW, 2 * LW))):
            moved = jnp.dot(pick, src[n, :, cols], preferred_element_type=F32)
            buf[n] = jnp.where(fresh, moved, buf[n].astype(F32)).astype(BF16)
        return carry

    def put(n, carry):
        for copy in stores(n, slots[n]):
            copy.start()
        return carry

    def finish(n, carry):
        for copy in stores(n, 0):
            copy.wait()
        return carry

    lax.fori_loop(0, count, update, 0)
    for copy in whole_copies:
        copy.wait()
    lax.fori_loop(0, count, put, 0)
    lax.fori_loop(0, count, finish, 0)


def patch(info, lens, table, news, key_cache, value_cache):
    shape = jax.ShapeDtypeStruct(key_cache.shape, BF16)
    return pl.pallas_call(
        patch_kernel,
        out_shape=(shape, shape, jax.ShapeDtypeStruct((1,), jnp.int32)),
        in_specs=[whole(SMEM)] * 3 + [whole(HBM)] * 4,
        out_specs=(whole(HBM), whole(HBM), whole(SMEM)),
        scratch_shapes=[
            VMEM((SLOTS, WINDOW, 2 * LW), BF16),
            VMEM((SLOTS, PT, LW), BF16),
            VMEM((SLOTS, PT, LW), BF16),
            pltpu.SemaphoreType.DMA((SLOTS, 6)),
            pltpu.SemaphoreType.DMA((2,)),
            SMEM((SLOTS,), jnp.int32),
            SMEM((SLOTS,), jnp.int32),
        ],
        compiler_params=pltpu.CompilerParams(vmem_limit_bytes=20 << 20),
        name="patch",
    )(info, lens, table, *news, key_cache, value_cache)


def shift(s):
    return [(i, (i + s) % 4) for i in range(4)]


PLANE = ("y", "x", "core")
CORES = [(0, 1), (1, 0)]


def plane_pairs(target, stage):
    pairs = []
    for y in range(4):
        for x in range(4):
            for c in range(2):
                along_x = (c == 0) == (stage == 0)
                to_y, to_x = (y, target(x)) if along_x else (target(y), x)
                pairs.append((y * 8 + x * 2 + c, to_y * 8 + to_x * 2 + c))
    return pairs


def send(array, s, stage):
    return lax.ppermute(array, PLANE, plane_pairs(lambda u: (u + s) % 4, stage))


def exchange(array, bits, stage):
    return lax.ppermute(array, PLANE, plane_pairs(lambda u: u ^ bits, stage))


def on_device(
    hidden,
    group_qkv,
    mlp_branch,
    key_cache,
    paged_value_cache,
    cache_lengths,
    page_table,
    dense_weight,
    dense_bias,
    norm_gain,
    norm_bias,
    qkv_weight,
    qkv_bias,
):
    y = lax.axis_index("y").astype(jnp.int32)
    x = lax.axis_index("x").astype(jnp.int32)
    core = lax.axis_index("core").astype(jnp.int32)
    head = lax.axis_index("head").astype(jnp.int32)
    page = 8 * y + 2 * x + core

    info = jnp.stack([page, y, x, core, head])

    inverse = 1.0 / 10000.0 ** (jnp.arange(0, ROT, 2, dtype=F32) / ROT)
    rates = jnp.broadcast_to(inverse[:, None], (ROT // 2, TOK))
    queries, fresh = rotary(info, cache_lengths, group_qkv, rates)

    other_keys = lax.ppermute(key_cache, "core", CORES)
    other_values = lax.ppermute(paged_value_cache, "core", CORES)
    other_fresh = lax.ppermute(fresh, "core", CORES)
    near = [queries] + [send(queries, s, 0) for s in range(1, 4)]
    codes, counts = page_lists(info, cache_lengths, page_table)
    pool_keys, pool_values = pool(other_keys, other_values)
    neighbour = exchange(fresh, 1, 0)
    near, codes, pool_keys, other_fresh, neighbour = lax.optimization_barrier(
        (near, codes, pool_keys, other_fresh, neighbour)
    )
    near = stack(near)
    all_queries = [near] + [send(near, s, 1) for s in range(1, 4)]

    caches = (key_cache, paged_value_cache, pool_keys, pool_values)

    pair = stack([fresh, neighbour])

    partials = [None] * 4
    last = None
    for s in (0, 1, 3, 2):
        wanted = all_queries[s]
        if last is not None:
            wanted, last = lax.optimization_barrier((wanted, last))
        if s == 1:
            wanted, pair = lax.optimization_barrier((wanted, pair))
            new_rows = stack([pair, exchange(pair, 3, 0)]).reshape(4, TOK, 2 * LW)
        if s == 2:
            wanted, new_rows = lax.optimization_barrier((wanted, new_rows))
        part = attend(
            s, info, cache_lengths, (codes, counts), wanted, caches, (fresh, other_fresh)
        )
        if last is not None:
            partials[before] = last if before == 0 else send(last, -before, 1)
        last, before = part, s
    partials[before] = send(last, -before, 1)
    blocks = join_rows(partials)
    blocks, new_rows = lax.optimization_barrier((blocks, new_rows))
    from_left = send(new_rows, 1, 1)
    from_right = send(new_rows, 3, 1)
    blocks = [blocks[0]] + [send(blocks[s], -s, 0) for s in range(1, 4)]
    attention = join_last(blocks)

    shares = dense(info, attention, dense_weight, dense_bias, hidden, mlp_branch)
    shares = [shares[0]] + [lax.ppermute(shares[s], "head", shift(s)) for s in range(1, 4)]
    from_left, from_right, _ = lax.optimization_barrier((from_left, from_right, shares[0]))
    opposite = send(from_left, 1, 1)
    news = [new_rows, from_left, opposite, from_right]
    new_hidden = join_shares(shares)
    news, _ = lax.optimization_barrier((news, new_hidden))
    gathered = stack(news)
    news = (gathered, lax.ppermute(gathered, "core", CORES))

    streams = [new_hidden] + [lax.ppermute(new_hidden, "head", shift(s)) for s in range(1, 4)]
    key_out, value_out, token = patch(
        info, cache_lengths, page_table, news, key_cache, paged_value_cache
    )
    late_weight, _ = lax.optimization_barrier((qkv_weight, new_hidden))
    next_qkv = project_qkv(
        info, token, streams, norm_gain, norm_bias, load(late_weight), qkv_bias
    )

    return (new_hidden, next_qkv, key_out, value_out)


def solution(mesh):
    plane = PLANE
    fine = Mesh(mesh.devices.reshape(4, 4, 4, 2), ("head",) + plane)
    in_specs = (
        P(plane, "head"),
        P(plane, "head"),
        P(plane, "head"),
        P(plane, None, "head"),
        P(plane, None, "head"),
        P(),
        P(),
        P("head", None),
        P(),
        P(),
        P(),
        P(None, "head"),
        P("head"),
    )
    out_specs = (
        P(plane, "head"),
        P(plane, "head"),
        P(plane, None, "head"),
        P(plane, None, "head"),
    )
    return jax.shard_map(
        on_device, mesh=fine, in_specs=in_specs, out_specs=out_specs, check_vma=False
    )
```
